128 devices in a mesh: lat: 16 (over y, x), lon: 8 (over z, core).
Axes of the slice: x: 4, y: 4, z: 4, core: 2. Of those that a mesh axis runs over, the one named last changes fastest.
Arguments:
- gaussian_thermal_state: float32 [16, 1280, 2560], P(None, 'lat', 'lon'), may hold values from -6 to 6
- radiation_holder_device: int32 [128, 6400, 1], P(('lat', 'lon')), may hold values from 0 to 127; in each aligned block of 6400 rows (0 to 6399, 6400 to 12799, ..., all dimensions but the last counted through in order) at most 80 rows name the same one
- layer_opacity_depths: bfloat16 [128, 16, 16, 10240], P(('lat', 'lon')), may hold values from 0.049804688 to 3
- wavenumber_duos_placed: int32 [640], replicated, may hold values from 0 to 639, each once
- reduced_grid_sites: int32 [1280], P('lat'), may hold values from 640 to 2560
- weighted_polynomial_basis: bfloat16 [640, 1280, 1344], P(('lat', 'lon')), may hold values from -0.15625 to 0.15625
Outputs:
- new_temperature: float32 [16, 1280, 2560], P(None, 'lat', 'lon')
The draws below stay inside these ranges and needn't reach their ends.
Inputs may be any that keep to these rules, and one draw needn't show every extreme that they name: `radiation_holder_device`: in each block d no owner is named by more than 80 of the block's 6400 columns; some owner is named by exactly 80 in some blocks. `wavenumber_duos_placed`: each pair number appears in exactly one slot.
All inputs are finite; a program needn't handle non-finite values.
Results may differ from the reference program's by a relative error of at most 0.0072.
Values may be sent and summed in bfloat16 or wider, within the bound.
No kernel may reach another device: no remote copies, remote signals or barrier semaphores. Data moves between devices by JAX's collectives and lax.ppermute only.
A program may use at most 192 MiB of HBM per device.

```python
import math
import jax
import jax.numpy as jnp
import numpy as np
from jax import lax

GAUSS_PARALLELS = 1280
MERIDIAN_TOTAL = 2560
BANDS = 16
NDEG = 1344
VERTICAL_LAYERS = 16
NWAVE = 1280
PAIRS = 640
CLAT = 40
CLON = 160
COLS_DEV = 6400
CAP = 80
N_LAT = 16
N_LON = 8
DEVICES = 128


def place_ends(entries, key, smallest, high):
    dims = entries.shape
    place = [jax.random.randint(jax.random.fold_in(key, axis), (), 0, dims[axis]) for axis in range(len(dims))]
    entries = entries.at[tuple(place)].set(smallest)
    longest = dims.index(max(dims))
    place[longest] = (place[longest] + 1) % dims[longest]
    return entries.at[tuple(place)].set(high)


def levels(rng, shape, cuts, least, high):
    level, own = 1.0, jax.random.fold_in(rng, 6)
    for dim, blocks in cuts:
        heights = jnp.exp(jax.random.uniform(jax.random.fold_in(own, dim), (blocks,), jnp.float32, least / len(cuts), high / len(cuts)))
        level = level * jnp.repeat(heights, shape[dim] // blocks).reshape([-1 if axis == dim else 1 for axis in range(len(shape))])
    return level


def deal_out(rng, own, number, rows, count, top, reach, lean):
    ranking = jax.random.permutation(rng, count)
    crowded, usual = portions_of(count, rows * top, reach, lean, True), portions_of(count, rows * top, reach, lean, False)
    places = jnp.arange(count)

    def named(sizes, turn):
        used = int((sizes > 0).sum())
        fixed = max(1, used // 4)
        moved = fixed + (places - fixed + turn * (used - fixed)) % max(1, count - fixed)
        return jnp.zeros((count,), jnp.int32).at[ranking[jnp.where(places < fixed, places, moved)]].set(jnp.asarray(sizes, jnp.int32))

    sizes = jnp.where(number % 4 == 0, named(crowded, number // 4), named(usual, number - number // 4 - 1))
    mixed = jax.random.permutation(jax.random.fold_in(own, 3), count)
    donor, taker = mixed[0:count // 2 * 2:2], mixed[1:count // 2 * 2:2]
    room = jnp.minimum(sizes[donor] - 1, reach - sizes[taker]) // 2
    room = jnp.where((donor == ranking[0]) | (taker == ranking[0]) | (sizes[taker] == 0), 0, jnp.maximum(room, 0))
    moved = jax.random.randint(jax.random.fold_in(own, 4), (count // 2,), 0, 1 << 20) % (room + 1)
    sizes = sizes.at[donor].add(-moved).at[taker].add(moved)
    items = jnp.searchsorted(jnp.cumsum(sizes), jnp.arange(rows * top), side="right").astype(jnp.int32)
    grid = items.reshape(top, rows).T
    grid = grid[jax.random.permutation(jax.random.fold_in(own, 1), rows)]
    turn = jax.random.randint(jax.random.fold_in(own, 2), (rows, 1), 0, top)
    return jnp.take_along_axis(grid, (jnp.arange(top)[None, :] + turn) % top, axis=1)


def portions_of(number_of, total, bound, lean, full):
    loads = [(1 << 20) // math.isqrt(standing ** lean) + 1 for standing in range(1, number_of + 1)]
    largest = bound if full else min(bound, max(-(-total // number_of), total * loads[0] // sum(loads)))
    least = 1 if total - largest >= number_of - 1 else 0
    holding, rest = [largest] + [least] * (number_of - 1), total - largest - least * (number_of - 1)
    while rest > 0:
        movable = [i for i in range(1, number_of) if holding[i] < largest] or [i for i in range(1, number_of) if holding[i] < bound]
        mass, budget = sum([loads[i] for i in movable]), rest
        for i in movable:
            addition = min(bound - holding[i], max(1, budget * loads[i] // mass), rest)
            holding[i] = holding[i] + addition
            rest = rest - addition
    return np.array(holding)


def scatter_about(key, extent, spread, most, cuts=(), kind=jnp.bfloat16):
    level = levels(key, extent, cuts, -0.22, 0.18) if cuts else 1.0
    values = jax.random.normal(key, extent, jnp.float32) * spread * level
    return jnp.minimum(jnp.maximum(values, -most), most).astype(kind)


def setup_inputs(seed: int = 0) -> dict:
    keys = jax.random.split(jax.random.key(seed), 7)
    gaussian_thermal_state = scatter_about(keys[0], (VERTICAL_LAYERS, GAUSS_PARALLELS, MERIDIAN_TOTAL), 1.0, 6.0, ((1, 16), (2, 8)), jnp.float32)
    radiation_holder_device_keys = jax.random.split(jax.random.fold_in(keys[1], 1), DEVICES * COLS_DEV // COLS_DEV)
    radiation_holder_device_turns = jax.random.permutation(jax.random.fold_in(keys[1], 3), DEVICES * COLS_DEV // COLS_DEV)
    radiation_holder_device = jax.vmap(lambda own, number: deal_out(jax.random.fold_in(keys[1], 2), own, number, COLS_DEV, DEVICES, 1, CAP, 2))(radiation_holder_device_keys, radiation_holder_device_turns).reshape((DEVICES, COLS_DEV, 1))
    layer_opacity_depths = jnp.clip(jnp.exp(math.log(3.0) - 4.0982585 * jax.random.uniform(keys[2], (DEVICES, VERTICAL_LAYERS, BANDS, DEVICES * CAP), jnp.float32) ** levels(keys[2], (DEVICES, VERTICAL_LAYERS, BANDS, DEVICES * CAP), ((0, 128),), -0.2, 0.2)), 0.049804688, 3.0).astype(jnp.bfloat16)
    wavenumber_duos_placed = jax.random.permutation(keys[3], PAIRS).astype(jnp.int32)
    reduced_grid_sites = place_ends(jax.random.randint(keys[4], (GAUSS_PARALLELS,), MERIDIAN_TOTAL // 4, MERIDIAN_TOTAL + 1), jax.random.fold_in(keys[4], 1), MERIDIAN_TOTAL // 4, MERIDIAN_TOTAL).astype(jnp.int32)
    weighted_polynomial_basis = scatter_about(keys[5], (PAIRS, GAUSS_PARALLELS, NDEG), GAUSS_PARALLELS ** -0.5, 0.15625, ((0, 128),))
    return dict(gaussian_thermal_state=gaussian_thermal_state, radiation_holder_device=radiation_holder_device, layer_opacity_depths=layer_opacity_depths, wavenumber_duos_placed=wavenumber_duos_placed, reduced_grid_sites=reduced_grid_sites, weighted_polynomial_basis=weighted_polynomial_basis)


DIFFUSION = 4.0

def wave_numbers(pairs, nwave):
    repeated = jnp.repeat(pairs, 4)
    which = jnp.tile(jnp.array([0, 0, 1, 1], dtype=jnp.int32), pairs.shape[0])
    return jnp.where(which == 0, repeated, nwave - 1 - repeated)

def dft_table(waves, nlon):
    places = jnp.arange(nlon, dtype=jnp.int32)
    phase = places[:, None] * waves[None, :] % nlon
    angle = phase.astype(jnp.float32) * (2.0 * math.pi / nlon)
    parity = jnp.arange(waves.shape[0], dtype=jnp.int32) % 2
    values = jnp.where(parity[None, :] == 0, jnp.cos(angle), jnp.sin(angle))
    return (values * (1.0 / math.sqrt(nlon))).astype(jnp.bfloat16)

def owner_ranks(owner, devices_all):
    matches = (owner[:, None] == jnp.arange(devices_all, dtype=jnp.int32)[None, :]).astype(jnp.int32)
    counts = lax.optimization_barrier(jnp.sum(matches, axis=0))
    starts = jnp.cumsum(counts) - counts
    start_each = lax.optimization_barrier(jnp.sum(matches * starts[None, :], axis=1))
    order = jnp.argsort(owner, stable=True)
    position = jnp.zeros_like(owner).at[order].set(jnp.arange(owner.shape[0], dtype=jnp.int32))
    return position - start_each

def flux_step(flux, inputs):
    passing, planck = inputs
    fresh = passing * flux + (1.0 - passing) * planck
    return (fresh, fresh)

def radiate(column_temp, depth):
    bands = depth.shape[1]
    source = jnp.exp(0.5 * column_temp.astype(jnp.float32))
    weights = (jnp.arange(bands, dtype=jnp.float32) + 1.0) * (2.0 / (bands * (bands + 1)))
    passing = jnp.exp(-depth.astype(jnp.float32))
    planck = weights[None, :, None] * source[:, None, :]
    _, below = lax.scan(flux_step, jnp.zeros_like(planck[0]), (passing, planck))
    above = jnp.concatenate([jnp.zeros_like(planck[:1]), below[:-1]], axis=0)
    _, upper = lax.scan(flux_step, planck[-1], (passing, planck), reverse=True)
    under = jnp.concatenate([upper[1:], planck[-1:]], axis=0)
    return lax.optimization_barrier(jnp.sum(above - below + under - upper, axis=1))

def reference(gaussian_thermal_state, radiation_holder_device, layer_opacity_depths, wavenumber_duos_placed, reduced_grid_sites, weighted_polynomial_basis):
    vertical_layer_pile = gaussian_thermal_state.shape[0]
    nwave = NWAVE
    reduced_resolution_grid = (gaussian_thermal_state[:, 0::2, 0::2] + gaussian_thermal_state[:, 1::2, 0::2] + (gaussian_thermal_state[:, 0::2, 1::2] + gaussian_thermal_state[:, 1::2, 1::2])) * 0.25
    reduced_resolution_grid = reduced_resolution_grid.astype(jnp.bfloat16)
    blocks = reduced_resolution_grid.reshape(vertical_layer_pile, N_LAT, CLAT, N_LON, CLON).transpose(1, 3, 0, 2, 4).reshape(DEVICES, vertical_layer_pile, CLAT * CLON)

    def block_heat(inputs):
        block_temp, block_owner, block_index = inputs
        owner = block_owner[:, 0]
        slots = block_index * CAP + owner_ranks(owner, DEVICES)
        depth = jnp.transpose(layer_opacity_depths[owner, :, :, slots], (1, 2, 0))
        return radiate(block_temp, depth).astype(jnp.bfloat16)
    heat_blocks = lax.map(block_heat, (blocks, radiation_holder_device, jnp.arange(DEVICES, dtype=jnp.int32)))
    coarse_heat = heat_blocks.reshape(N_LAT, N_LON, vertical_layer_pile, CLAT, CLON).transpose(2, 0, 3, 1, 4).reshape(vertical_layer_pile, GAUSS_PARALLELS // 2, MERIDIAN_TOTAL // 2)
    full_resolution_warming = jnp.repeat(jnp.repeat(coarse_heat, 2, axis=1), 2, axis=2)
    radiatively_driven_thermal = (gaussian_thermal_state + full_resolution_warming.astype(jnp.float32)).astype(jnp.bfloat16)
    waves = wave_numbers(wavenumber_duos_placed, nwave)
    table = dft_table(waves, MERIDIAN_TOTAL)
    ncol = waves.shape[0]
    fourier = jnp.dot(radiatively_driven_thermal.reshape(vertical_layer_pile * GAUSS_PARALLELS, MERIDIAN_TOTAL), table, preferred_element_type=jnp.float32).reshape(vertical_layer_pile, GAUSS_PARALLELS, ncol)
    keep = 2 * waves[None, :] < reduced_grid_sites[:, None]
    fourier = jnp.where(keep[None], fourier, 0.0).astype(jnp.bfloat16)
    right_all = fourier.reshape(vertical_layer_pile, GAUSS_PARALLELS, PAIRS, 4).transpose(2, 0, 1, 3)
    coeff = jnp.arange(NDEG, dtype=jnp.int32)

    def per_slot(inputs):
        basis, right, pair = inputs
        right = right.reshape(vertical_layer_pile, GAUSS_PARALLELS, 2, 2).transpose(1, 2, 0, 3).reshape(GAUSS_PARALLELS, 4 * vertical_layer_pile)
        full = lax.dot_general(basis, right, (((0,), (0,)), ((), ())), preferred_element_type=jnp.float32)
        full = full.reshape(NDEG, 2, 2 * vertical_layer_pile)
        first = coeff < nwave - pair
        chosen = jnp.where(first[:, None], full[:, 0], full[:, 1])
        degree = jnp.where(first, pair + coeff, coeff - 1).astype(jnp.float32)
        factor = jnp.where(coeff <= nwave, 1.0 / (1.0 + DIFFUSION * degree * (degree + 1.0) / (nwave * nwave)), 0.0)
        damped = (chosen * factor[:, None]).astype(jnp.bfloat16)
        blank = jnp.zeros_like(damped)
        split = jnp.stack([jnp.where(first[:, None], damped, blank), jnp.where(first[:, None], blank, damped)], axis=1)
        synth = jnp.dot(basis, split.reshape(NDEG, 4 * vertical_layer_pile), preferred_element_type=jnp.float32)
        return synth.astype(jnp.bfloat16)
    synth_all = lax.map(per_slot, (weighted_polynomial_basis, right_all, wavenumber_duos_placed))
    synth = synth_all.reshape(PAIRS, GAUSS_PARALLELS, 2, vertical_layer_pile, 2).transpose(3, 1, 0, 2, 4).reshape(vertical_layer_pile * GAUSS_PARALLELS, ncol)
    result = lax.dot_general(synth, table, (((1,), (1,)), ((), ())), preferred_element_type=jnp.float32)
    return result.reshape(vertical_layer_pile, GAUSS_PARALLELS, MERIDIAN_TOTAL)
```

```python
import functools
import math

import jax
import jax.numpy as jnp
from jax import lax
from jax.experimental import pallas as pl
from jax.experimental.pallas import tpu as pltpu
from jax.sharding import PartitionSpec as P

DIFFUSION = 4.0
BF16 = jnp.bfloat16
F32 = jnp.float32
I32 = jnp.int32
ALL = ("lat", "lon")
NT = (((1,), (1,)), ((), ()))


def iota(shape, dim):
    return lax.broadcasted_iota(I32, shape, dim)


def mm(a, b):
    return jnp.dot(a, b, preferred_element_type=F32)


def split_mm_right(x, b):
    hi = x.astype(BF16)
    lo = (x - hi.astype(F32)).astype(BF16)
    return mm(hi, b) + mm(lo, b)


def split_mm_left(a, x):
    hi = x.astype(BF16)
    lo = (x - hi.astype(F32)).astype(BF16)
    return mm(a, hi) + mm(a, lo)


def pack_kernel(state_ref, owner_ref, out_ref, code_ref, coarse, owners, values, total):
    levels, lines, width = state_ref.shape
    rows, lanes = owner_ref.shape
    devices = 128
    low = 16
    high = out_ref.shape[0] // devices
    pool_y = (iota((rows, lines), 1) // 2 == iota((rows, lines), 0)).astype(F32).astype(BF16)
    pool_x = (iota((width, lanes), 0) // 2 == iota((width, lanes), 1)).astype(F32).astype(BF16)

    def pool(level, carry):
        summed = split_mm_left(pool_y, state_ref[level])
        mean = 0.25 * split_mm_right(summed, pool_x)
        coarse[level] = mean.astype(BF16).astype(F32)
        return carry

    lax.fori_loop(0, levels, pool, 0)
    wide = lanes + devices
    before = (
        (iota((lanes, wide), 0) < iota((lanes, wide), 1)) | (iota((lanes, wide), 1) >= lanes)
    ).astype(F32).astype(BF16)
    total[...] = jnp.zeros_like(total)

    def chunk(c, base):
        start = pl.multiple_of(c * 8, 8)
        owner8 = owner_ref[pl.ds(start, 8), :]
        ranks = []
        for u in range(8):
            here = owner8[u : u + 1, :]
            match = (iota((devices, lanes), 0) == here).astype(F32)
            counted = mm(match.astype(BF16), before)
            both = jnp.concatenate([base, base], axis=1)
            rank = jnp.sum(match * (counted[:, :lanes] + both), axis=0, keepdims=True)
            base = base + counted[:, lanes:]
            rank = rank.astype(I32)
            ranks.append(here * 128 + rank)
            span = slice(u * lanes, (u + 1) * lanes)
            for h in range(high):
                part = ((rank // low) == h).astype(F32)
                owners[h * devices : (h + 1) * devices, span] = (match * part).astype(BF16)
            slot = (iota((low, lanes), 0) == rank % low).astype(F32)
            for level in range(levels):
                line = coarse[level, pl.ds(start, 8), :][u : u + 1, :]
                values[level * low : (level + 1) * low, span] = (slot * line).astype(BF16)
        code_ref[pl.ds(start, 8), :] = jnp.concatenate(ranks, axis=0)
        total[...] += lax.dot_general(
            owners[...], values[...], NT, preferred_element_type=F32
        )
        return base

    lax.fori_loop(0, rows // 8, chunk, jnp.zeros((devices, devices), F32))
    out_ref[...] = total[...].astype(BF16)


def pack(state, owner):
    levels = state.shape[0]
    rows, lanes = owner.shape
    return pl.pallas_call(
        pack_kernel,
        out_shape=(
            jax.ShapeDtypeStruct((640, levels * 16), BF16),
            jax.ShapeDtypeStruct((rows, lanes), I32),
        ),
        scratch_shapes=[
            pltpu.VMEM((levels, rows, lanes), F32),
            pltpu.VMEM((640, 8 * lanes), BF16),
            pltpu.VMEM((levels * 16, 8 * lanes), BF16),
            pltpu.VMEM((640, levels * 16), F32),
        ],
        compiler_params=pltpu.CompilerParams(vmem_limit_bytes=24 * 2**20),
        name="pack",
    )(state, owner)


def radiate_kernel(came_ref, depth_ref, out_ref, temp, lost, down, heat):
    blocks, levels, cap = came_ref.shape
    bands = depth_ref.shape[1]
    for j in range(blocks):
        temp[:, j * cap : (j + 1) * cap] = came_ref[j].astype(F32)
    temp[...] = jnp.exp(0.5 * temp[...])
    weight = (iota((bands, 1), 0).astype(F32) + 1.0) * (2.0 / (bands * (bands + 1)))
    flux = jnp.zeros((bands, blocks * cap), F32)
    for level in range(levels):
        share = 1.0 - jnp.exp(-depth_ref[level].astype(F32))
        lost[level] = share
        step = share * (flux - temp[level : level + 1, :])
        down[level] = step
        flux = flux - step
    flux = jnp.broadcast_to(temp[levels - 1 : levels, :], flux.shape)
    for level in reversed(range(levels)):
        step = lost[level] * (flux - temp[level : level + 1, :])
        flux = flux - step
        heat[level : level + 1, :] = jnp.sum(
            (step + down[level]) * weight, axis=0, keepdims=True
        )
    group = out_ref.shape[1]
    for b in range(levels // group):
        out_ref[b] = heat[b * group : (b + 1) * group, :].astype(BF16)


def radiate(came, depth, lat_size, lon_size):
    devices, levels, cap = came.shape
    bands = depth.shape[1]
    width = lon_size * cap
    group = levels // lon_size
    return pl.pallas_call(
        radiate_kernel,
        grid=(lat_size,),
        out_shape=jax.ShapeDtypeStruct((devices, group, width), BF16),
        in_specs=[
            pl.BlockSpec((lon_size, levels, cap), lambda a: (a, 0, 0)),
            pl.BlockSpec((levels, bands, width), lambda a: (0, 0, a)),
        ],
        out_specs=pl.BlockSpec((lon_size, group, width), lambda a: (a, 0, 0)),
        scratch_shapes=[
            pltpu.VMEM((levels, width), F32),
            pltpu.VMEM((levels, bands, width), F32),
            pltpu.VMEM((levels, bands, width), F32),
            pltpu.VMEM((levels, width), F32),
        ],
        compiler_params=pltpu.CompilerParams(vmem_limit_bytes=16 * 2**20),
        name="radiate",
    )(came, depth)


def turns(count, whole):
    quarter = jnp.floor(count * (4.0 / whole) + 0.5)
    angle = (count - quarter * (whole / 4.0)) * (2.0 * math.pi / whole)
    sq = angle * angle
    sin = angle * (1.0 + sq * (-1.0 / 6.0 + sq * (1.0 / 120.0 + sq * (-1.0 / 5040.0))))
    cos = 1.0 + sq * (-0.5 + sq * (1.0 / 24.0 + sq * (-1.0 / 720.0 + sq * (1.0 / 40320.0))))
    side = quarter.astype(I32) & 3
    odd = (side & 1) == 1
    real = jnp.where(odd, sin, cos)
    imag = jnp.where(odd, cos, sin)
    real = jnp.where((side == 1) | (side == 2), -real, real)
    imag = jnp.where(side >= 2, -imag, imag)
    return real, imag


def table_kernel(nwave, pair_ref, fine_ref, coarse_ref):
    devices = pair_ref.shape[1]
    nlon = fine_ref.shape[3]
    scale = 1.0 / math.sqrt(nlon)
    step_rows = 16
    lane = iota((step_rows, 128), 1).astype(F32)
    lane_i = iota((step_rows, 128), 1)
    tail0 = ((lane_i // 32) * 160 + 128 + lane_i % 32).astype(F32)

    def block(i, carry):
        rows = pl.ds(pl.multiple_of(i * step_rows, step_rows), step_rows)
        for h in range(2):
            pair = pair_ref[0, rows, :].astype(F32)
            wave = pair if h == 0 else (nwave - 1.0) - pair
            wave = jnp.broadcast_to(wave, (step_rows, 128))
            c, s = turns(wave * lane, float(nlon))
            c, s = c * scale, s * scale
            rc, rs = turns(wave * 128.0, float(nlon))
            for t in range(nlon // 128):
                fine_ref[0, 2 * h, rows, t * 128 : (t + 1) * 128] = c.astype(BF16)
                fine_ref[0, 2 * h + 1, rows, t * 128 : (t + 1) * 128] = s.astype(BF16)
                c, s = c * rc - s * rs, s * rc + c * rs
            amp, _ = turns(wave, 2.0 * nlon)
            amp = amp * (2.0 * scale)
            c, s = turns(wave * (4.0 * lane + 1.0), 2.0 * nlon)
            c, s = c * amp, s * amp
            rc, rs = turns(wave * 640.0, 2.0 * nlon)
            for t in range(8):
                coarse_ref[0, 2 * h, rows, t * 128 : (t + 1) * 128] = c.astype(BF16)
                coarse_ref[0, 2 * h + 1, rows, t * 128 : (t + 1) * 128] = s.astype(BF16)
                c, s = c * rc - s * rs, s * rc + c * rs
            c, s = turns(wave * (4.0 * tail0 + 1.0), 2.0 * nlon)
            c, s = c * amp, s * amp
            rc, rs = turns(wave * 2560.0, 2.0 * nlon)
            for t in range(8, 10):
                coarse_ref[0, 2 * h, rows, t * 128 : (t + 1) * 128] = c.astype(BF16)
                coarse_ref[0, 2 * h + 1, rows, t * 128 : (t + 1) * 128] = s.astype(BF16)
                c, s = c * rc - s * rs, s * rc + c * rs
        return carry

    lax.fori_loop(0, devices // step_rows, block, 0)


def tables(pairs, nwave, nlon):
    group, devices, _ = pairs.shape
    return pl.pallas_call(
        functools.partial(table_kernel, nwave),
        grid=(group,),
        out_shape=(
            jax.ShapeDtypeStruct((group, 4, devices, nlon), BF16),
            jax.ShapeDtypeStruct((group, 4, devices, nlon // 2), BF16),
        ),
        in_specs=[pl.BlockSpec((1, devices, 1), lambda s: (s, 0, 0))],
        out_specs=(
            pl.BlockSpec((1, 4, devices, nlon), lambda s: (s, 0, 0, 0)),
            pl.BlockSpec((1, 4, devices, nlon // 2), lambda s: (s, 0, 0, 0)),
        ),
        compiler_params=pltpu.CompilerParams(vmem_limit_bytes=16 * 2**20),
        name="tables",
    )(pairs)


def fourier_kernel(piece_ref, fine_ref, out_ref, rows):
    blocks, group, lines, width = piece_ref.shape
    nlon = rows.shape[1]

    @pl.when(pl.program_id(0) == 0)
    def _():
        rows[...] = jnp.zeros_like(rows)
        for g in range(group):
            for j in range(blocks):
                rows[g * 128 : g * 128 + lines, j * width : (j + 1) * width] = piece_ref[j, g]

    out_ref[0] = lax.dot_general(
        fine_ref[0].reshape(out_ref.shape[1], nlon), rows[...], NT, preferred_element_type=F32
    )


def fourier(piece, fine):
    group, four, devices, nlon = fine.shape
    levels = piece.shape[1]
    return pl.pallas_call(
        fourier_kernel,
        grid=(group,),
        out_shape=jax.ShapeDtypeStruct((group, four * devices, levels * 128), F32),
        in_specs=[
            pl.BlockSpec(piece.shape, lambda s: (0, 0, 0, 0)),
            pl.BlockSpec((1, four, devices, nlon), lambda s: (s, 0, 0, 0)),
        ],
        out_specs=pl.BlockSpec((1, four * devices, levels * 128), lambda s: (s, 0, 0)),
        scratch_shapes=[pltpu.VMEM((levels * 128, nlon), BF16)],
        compiler_params=pltpu.CompilerParams(vmem_limit_bytes=16 * 2**20),
        name="fourier",
    )(piece, fine)


def unpack_kernel(came_ref, code_ref, out_ref, heat):
    blocks, groups = code_ref.shape[0], code_ref.shape[1]
    levels, width, devices = came_ref.shape
    cap = width // blocks
    lines = heat.shape[1] // levels
    for j in range(blocks):

        def pick(g, carry):
            code = code_ref[j, g]
            for q in range(5):
                row = code[q : q + 1, :]
                owner = jnp.broadcast_to(row // 128, (8, 128))
                rank = jnp.broadcast_to(row % 128, (8, 128))
                for level in range(levels):
                    found = jnp.zeros((8, 128), F32)
                    for t in range(cap // 8):
                        here = came_ref[level, j * cap + 8 * t : j * cap + 8 * t + 8, :]
                        got = jnp.take_along_axis(
                            here, owner, axis=1, mode="promise_in_bounds"
                        )
                        found = jnp.where(rank // 8 == t, got, found)
                    found = jnp.where(rank % 8 == iota((8, 128), 0), found, 0.0)
                    value = jnp.sum(found, axis=0, keepdims=True)
                    if q < 4:
                        heat[j, pl.ds(level * lines + 4 * g + q, 1), :] = value
                    else:
                        tile = blocks + j // 4
                        mine = iota((1, 128), 1) // 32 == j % 4
                        for i in range(4):
                            moved = pltpu.roll(value, (32 * (j % 4 - i)) % 128, 1)
                            at = pl.ds(level * lines + 4 * g + i, 1)
                            heat[tile, at, :] = jnp.where(mine, moved, heat[tile, at, :])
            return carry

        lax.fori_loop(0, groups, pick, 0)
    for t in range(heat.shape[0]):
        out_ref[:, t * 128 : (t + 1) * 128] = heat[t].astype(BF16)


def unpack(came, code):
    levels, width, devices = came.shape
    blocks, groups = code.shape[0], code.shape[1]
    shape = (levels * groups * 4, blocks * 160)
    return pl.pallas_call(
        unpack_kernel,
        out_shape=jax.ShapeDtypeStruct(shape, BF16),
        scratch_shapes=[pltpu.VMEM((shape[1] // 128, shape[0], 128), F32)],
        compiler_params=pltpu.CompilerParams(vmem_limit_bytes=16 * 2**20),
        name="unpack",
    )(came, code)


def heated_kernel(nwave, heat_ref, coarse_ref, base_ref, pair_ref, sites_ref, out_ref, rows, mixed):
    step = pl.program_id(0)
    devices = pair_ref.shape[1]
    lines = heat_ref.shape[0] // 2
    cap = 80

    @pl.when(step == 0)
    def _():
        twice = iota((256, 2 * lines), 0)
        source = (twice // 128) * lines + (twice % 128) // 2
        keep = (source == iota((256, 2 * lines), 1)) & (twice % 128 < 2 * lines)
        rows[...] = mm(keep.astype(F32).astype(BF16), heat_ref[...]).astype(BF16)

    product = base_ref[0] + lax.dot_general(
        coarse_ref[0].reshape(4 * devices, rows.shape[1]),
        rows[...],
        NT,
        preferred_element_type=F32,
    )
    pair = pair_ref[0]
    for k in range(4):
        wave = pair if k < 2 else nwave - 1 - pair
        part = jnp.where(
            2 * wave < sites_ref[...], product[k * devices : (k + 1) * devices, :], 0.0
        )
        for level in range(2):
            mixed[pl.ds(level * 4 + k, devices, stride=8), :] = part[
                :, level * 128 : (level + 1) * 128
            ]
    for k in range(5):

        @pl.when(step == k)
        def _(k=k):
            out_ref[:, :, k * cap : (k + 1) * cap] = (
                mixed[...].reshape(devices, 8, 128)[:, :, :cap].astype(BF16)
            )


def heated(heat, coarse, base, pairs, sites, nwave):
    group, four, devices, half = coarse.shape
    return pl.pallas_call(
        functools.partial(heated_kernel, nwave),
        grid=(group,),
        out_shape=jax.ShapeDtypeStruct((devices, 8, group * 80), BF16),
        in_specs=[
            pl.BlockSpec(heat.shape, lambda s: (0, 0)),
            pl.BlockSpec((1, four, devices, half), lambda s: (s, 0, 0, 0)),
            pl.BlockSpec((1, four * devices, base.shape[2]), lambda s: (s, 0, 0)),
            pl.BlockSpec((1, devices, 1), lambda s: (s, 0, 0)),
            pl.BlockSpec(sites.shape, lambda s: (0, 0)),
        ],
        out_specs=pl.BlockSpec((devices, 8, group * 80), lambda s: (0, 0, 0)),
        scratch_shapes=[
            pltpu.VMEM((256, half), BF16),
            pltpu.VMEM((devices * 8, 128), F32),
        ],
        compiler_params=pltpu.CompilerParams(vmem_limit_bytes=16 * 2**20),
        name="heated",
    )(heat, coarse, base, pairs, sites)


def legendre_kernel(nwave, pair_ref, came_ref, basis_ref, out_ref, right):
    step = pl.program_id(0)
    nlat, ndeg = basis_ref.shape[1], basis_ref.shape[2]
    bands = nlat // 80
    for k in range(5):

        @pl.when(step == k)
        def _(k=k):
            for a in range(bands):
                block = came_ref[a * 8 : (a + 1) * 8, :, k * 80 : (k + 1) * 80].astype(F32)
                right[:, a * 80 : (a + 1) * 80] = block.reshape(64, 80).astype(BF16)

    pair = pair_ref[step]
    full = mm(right[...], basis_ref[0])
    coeff = iota((64, ndeg), 1)
    head = (iota((64, ndeg), 0) % 4) < 2
    first = coeff < nwave - pair
    degree = jnp.where(first, pair + coeff, coeff - 1).astype(F32)
    factor = 1.0 / (1.0 + DIFFUSION * degree * (degree + 1.0) / (nwave * nwave))
    keep = (first & head) | (jnp.logical_not(first) & jnp.logical_not(head) & (coeff <= nwave))
    damped = jnp.where(keep, full * factor, 0.0).astype(BF16)
    synth = lax.dot_general(damped, basis_ref[0], NT, preferred_element_type=F32)
    for k in range(5):

        @pl.when(step == k)
        def _(k=k):
            for a in range(bands):
                block = synth[:, a * 80 : (a + 1) * 80].reshape(8, 8, 80)
                out_ref[a * 8 : (a + 1) * 8, :, k * 80 : (k + 1) * 80] = block.astype(BF16)


def legendre(pairs, came, basis, nwave):
    group, nlat, ndeg = basis.shape
    return pl.pallas_call(
        functools.partial(legendre_kernel, nwave),
        grid_spec=pltpu.PrefetchScalarGridSpec(
            num_scalar_prefetch=1,
            grid=(group,),
            in_specs=[
                pl.BlockSpec(came.shape, lambda s, p: (0, 0, 0)),
                pl.BlockSpec((1, nlat, ndeg), lambda s, p: (s, 0, 0)),
            ],
            out_specs=pl.BlockSpec(came.shape, lambda s, p: (0, 0, 0)),
            scratch_shapes=[pltpu.VMEM((64, nlat), BF16)],
        ),
        out_shape=jax.ShapeDtypeStruct(came.shape, BF16),
        compiler_params=pltpu.CompilerParams(vmem_limit_bytes=24 * 2**20),
        name="legendre",
    )(pairs, came, basis)


def inverse_kernel(came_ref, fine_ref, out_ref, mixed, left, total):
    step = pl.program_id(0)
    devices = came_ref.shape[0]
    blocks, lines2, width = out_ref.shape
    for k in range(5):

        @pl.when(step == k)
        def _(k=k):
            mixed[:, :80] = (
                came_ref[:, :, k * 80 : (k + 1) * 80].astype(F32).reshape(devices * 8, 80)
            )

    for k in range(4):
        for level in range(2):
            part = mixed[pl.ds(level * 4 + k, devices, stride=8), :]
            left[level * 80 : (level + 1) * 80, k * devices : (k + 1) * devices] = part.T[
                :80, :
            ].astype(BF16)
    product = mm(left[...], fine_ref[0].reshape(4 * devices, total.shape[1]))

    @pl.when(step == 0)
    def _():
        total[...] = product

    @pl.when(step > 0)
    def _():
        total[...] += product

    @pl.when(step == pl.num_programs(0) - 1)
    def _():
        for j in range(blocks):
            out_ref[j] = total[:, j * width : (j + 1) * width].astype(BF16)


def inverse(came, fine, blocks):
    group, four, devices, nlon = fine.shape
    return pl.pallas_call(
        inverse_kernel,
        grid=(group,),
        out_shape=jax.ShapeDtypeStruct((blocks, 160, nlon // blocks), BF16),
        in_specs=[
            pl.BlockSpec(came.shape, lambda s: (0, 0, 0)),
            pl.BlockSpec((1, four, devices, nlon), lambda s: (s, 0, 0, 0)),
        ],
        out_specs=pl.BlockSpec((blocks, 160, nlon // blocks), lambda s: (0, 0, 0)),
        scratch_shapes=[
            pltpu.VMEM((devices * 8, 128), F32),
            pltpu.VMEM((160, four * devices), BF16),
            pltpu.VMEM((160, nlon), F32),
        ],
        compiler_params=pltpu.CompilerParams(vmem_limit_bytes=24 * 2**20),
        name="inverse",
    )(came, fine)


def swap(x, axes):
    return lax.all_to_all(x, axes, split_axis=0, concat_axis=0, tiled=True)


def per_device(state, holder, depths, pairs, sites, basis):
    levels, lines, width = state.shape
    group, nlat, ndeg = basis.shape
    nwave = pairs.shape[0] * 2
    nlon = nwave * 2
    lat_size = lax.axis_size("lat")
    lon_size = lax.axis_size("lon")
    devices = lat_size * lon_size
    level_group = levels // lon_size
    rows, cols = lines // 2, width // 2
    me = lax.axis_index("lat") * lon_size + lax.axis_index("lon")

    piece = swap(state.astype(BF16), "lon").reshape(lon_size, level_group, lines, width)

    owner = jnp.pad(holder.reshape(rows, cols), ((0, 0), (0, 256 - cols)), constant_values=-1)
    sorted_cols, code = pack(state, owner)
    outgoing = sorted_cols.reshape(5, devices, levels, 16).transpose(1, 2, 0, 3)
    came = swap(outgoing.reshape(devices, levels, 80), ALL)
    code = jnp.concatenate(
        [
            code[:, :128].reshape(rows // 4, 4, 128),
            code[:, 128:160].reshape(rows // 4, 1, 128),
            jnp.zeros((rows // 4, 3, 128), I32),
        ],
        axis=1,
    )
    codes = swap(jnp.broadcast_to(code[None], (lon_size,) + code.shape), "lon")

    slots = pairs.reshape(devices, group).T[:, :, None]
    fine, coarse = tables(slots, nwave, nlon)
    base = fourier(piece, fine)

    heat = radiate(came, depths[0], lat_size, lon_size)
    returned = swap(heat, ALL).transpose(1, 2, 0).astype(F32)
    warm = unpack(returned, codes)
    limits = jnp.pad(sites, (0, 128 - lines))
    limits = jnp.concatenate([limits, limits])[None, :]
    sending = heated(warm, coarse, base, slots, limits, nwave)
    arrived = swap(sending, ALL)
    mine = lax.dynamic_slice_in_dim(pairs, me * group, group)
    back = swap(legendre(mine, arrived, basis, nwave), ALL)
    grid = swap(inverse(back, fine, lon_size), "lon")
    return grid.reshape(levels, lines, width).astype(F32)


def solution(mesh):
    in_specs = (
        P(None, "lat", "lon"),
        P(("lat", "lon"), None, None),
        P(("lat", "lon"), None, None, None),
        P(),
        P("lat"),
        P(("lat", "lon"), None, None),
    )
    out_specs = P(None, "lat", "lon")
    return jax.shard_map(
        per_device, mesh=mesh, in_specs=in_specs, out_specs=out_specs, check_vma=False
    )
```

```python
import functools
import math

import jax
import jax.numpy as jnp
from jax import lax
from jax.experimental import pallas as pl
from jax.experimental.pallas import tpu as pltpu
from jax.sharding import PartitionSpec as P


DIFFUSION = 4.0
BF16 = jnp.bfloat16
F32 = jnp.float32
I32 = jnp.int32
ALL = ("lat", "lon")
NT = (((1,), (1,)), ((), ()))


def iota(shape, dim):
    return lax.broadcasted_iota(I32, shape, dim)


def mm(a, b):
    return jnp.dot(a, b, preferred_element_type=F32)


def split_mm_right(x, b):
    hi = x.astype(BF16)
    lo = (x - hi.astype(F32)).astype(BF16)
    return mm(hi, b) + mm(lo, b)


def pack_kernel(state_ref, owner_ref, out_ref, code_ref, halves, coarse, marks, owners, values, total):
    levels, lines, width = state_ref.shape
    rows, lanes = owner_ref.shape
    devices = 128
    low = 16
    high = out_ref.shape[0] // devices
    pool_x = (iota((width, lanes), 0) // 2 == iota((width, lanes), 1)).astype(F32).astype(BF16)
    summed = split_mm_right(state_ref[...].reshape(levels * lines, width), pool_x)
    for t in range(2):
        halves[t] = summed[:, t * 128 : (t + 1) * 128]
    for level in range(levels):
        for t in range(2):
            even = halves[t, pl.ds(level * lines, rows, stride=2), :]
            odd = halves[t, pl.ds(level * lines + 1, rows, stride=2), :]
            mean = 0.25 * (even + odd)
            coarse[level, :, t * 128 : (t + 1) * 128] = mean.astype(BF16).astype(F32)
    before = (iota((lanes, lanes), 0) < iota((lanes, lanes), 1)).astype(F32).astype(BF16)
    total[...] = jnp.zeros_like(total)
    short = iota((8, 128), 1) < 32

    def tails(x):
        moved = x
        for i in range(1, 4):
            moved = jnp.where(iota((8, 128), 0) % 4 == i, pltpu.roll(x, 32 * i, 1), moved)
        return [jnp.sum(moved[4 * i : 4 * i + 4, :], axis=0, keepdims=True) for i in range(2)]

    def chunk(c, base):
        start = pl.multiple_of(c * 8, 8)
        owner8 = owner_ref[pl.ds(start, 8), :]
        for u in range(8):
            match = (iota((devices, lanes), 0) == owner8[u : u + 1, :]).astype(F32)
            marks[u * devices : (u + 1) * devices, :] = match.astype(BF16)
        counted = mm(marks[...], before)
        ranks = []
        for u in range(8):
            here = counted[u * devices : (u + 1) * devices, :]
            match = (iota((devices, lanes), 0) == owner8[u : u + 1, :]).astype(F32)
            both = jnp.concatenate([base, base], axis=1)
            ranks.append(jnp.sum(match * (here + both), axis=0, keepdims=True))
            base = base + here[:, lanes - 1 : lanes]
        code = owner8 * 128 + jnp.concatenate(ranks, axis=0).astype(I32)
        ends = tails(jnp.where(short, code[:, 128:], 0))
        for i in range(2):
            code_ref[2 * c + i] = jnp.concatenate(
                [code[4 * i : 4 * i + 4, :128], ends[i], jnp.zeros((3, 128), I32)], axis=0
            )
        lines8 = [code[u : u + 1, :128] for u in range(8)] + ends
        temps = []
        for level in range(levels):
            block = coarse[level, pl.ds(start, 8), :]
            temps.append([block[u : u + 1, :128] for u in range(8)] + tails(block[:, 128:]))
        for u in range(10):
            span = slice(u * 128, (u + 1) * 128)
            owner = lines8[u] // 128
            rank = lines8[u] % 128
            match = (iota((devices, 128), 0) == owner).astype(F32)
            for h in range(high):
                part = ((rank // low) == h).astype(F32)
                owners[h * devices : (h + 1) * devices, span] = (match * part).astype(BF16)
            slot = (iota((low, 128), 0) == rank % low).astype(F32)
            for level in range(levels):
                values[level * low : (level + 1) * low, span] = (
                    slot * temps[level][u]
                ).astype(BF16)
        total[...] += lax.dot_general(
            owners[...], values[...], NT, preferred_element_type=F32
        )
        return base

    lax.fori_loop(0, rows // 8, chunk, jnp.zeros((devices, devices), F32))
    out_ref[...] = total[...].astype(BF16)


def pack(state, owner):
    levels, lines, _ = state.shape
    rows, lanes = owner.shape
    return pl.pallas_call(
        pack_kernel,
        out_shape=(
            jax.ShapeDtypeStruct((640, levels * 16), BF16),
            jax.ShapeDtypeStruct((rows // 4, 8, 128), I32),
        ),
        scratch_shapes=[
            pltpu.VMEM((2, levels * lines, 128), F32),
            pltpu.VMEM((levels, rows, lanes), F32),
            pltpu.VMEM((8 * 128, lanes), BF16),
            pltpu.VMEM((640, 1280), BF16),
            pltpu.VMEM((levels * 16, 1280), BF16),
            pltpu.VMEM((640, levels * 16), F32),
        ],
        compiler_params=pltpu.CompilerParams(vmem_limit_bytes=20 * 2**20),
        cost_estimate=pl.CostEstimate(flops=6 * 10**9, bytes_accessed=2 * 10**6, transcendentals=0),
        name="pack",
    )(state, owner)


def radiate_kernel(came_ref, depth_ref, out_ref, temp, lost, down, heat):
    blocks, levels, cap = came_ref.shape
    bands = depth_ref.shape[1]
    for j in range(blocks):
        temp[:, j * cap : (j + 1) * cap] = came_ref[j].astype(F32)
    temp[...] = jnp.exp(0.5 * temp[...])
    weight = (iota((bands, 1), 0).astype(F32) + 1.0) * (2.0 / (bands * (bands + 1)))
    flux = jnp.zeros((bands, blocks * cap), F32)
    for level in range(levels):
        share = 1.0 - jnp.exp(-depth_ref[level].astype(F32))
        lost[level] = share
        step = share * (flux - temp[level : level + 1, :])
        down[level] = step
        flux = flux - step
    flux = jnp.broadcast_to(temp[levels - 1 : levels, :], flux.shape)
    for level in reversed(range(levels)):
        step = lost[level] * (flux - temp[level : level + 1, :])
        flux = flux - step
        heat[level : level + 1, :] = jnp.sum(
            (step + down[level]) * weight, axis=0, keepdims=True
        )
    group = out_ref.shape[1]
    for b in range(levels // group):
        out_ref[b] = heat[b * group : (b + 1) * group, :].astype(BF16)


def radiate(came, depth, lat_size, lon_size):
    devices, levels, cap = came.shape
    bands = depth.shape[1]
    width = lon_size * cap
    group = levels // lon_size
    return pl.pallas_call(
        radiate_kernel,
        grid=(lat_size,),
        out_shape=jax.ShapeDtypeStruct((devices, group, width), BF16),
        in_specs=[
            pl.BlockSpec((lon_size, levels, cap), lambda a: (a, 0, 0)),
            pl.BlockSpec((levels, bands, width), lambda a: (0, 0, a)),
        ],
        out_specs=pl.BlockSpec((lon_size, group, width), lambda a: (a, 0, 0)),
        scratch_shapes=[
            pltpu.VMEM((levels, width), F32),
            pltpu.VMEM((levels, bands, width), F32),
            pltpu.VMEM((levels, bands, width), F32),
            pltpu.VMEM((levels, width), F32),
        ],
        compiler_params=pltpu.CompilerParams(vmem_limit_bytes=16 * 2**20),
        name="radiate",
    )(came, depth)


def turns(count, whole):
    quarter = jnp.floor(count * (4.0 / whole) + 0.5)
    angle = (count - quarter * (whole / 4.0)) * (2.0 * math.pi / whole)
    sq = angle * angle
    sin = angle * (1.0 + sq * (-1.0 / 6.0 + sq * (1.0 / 120.0 + sq * (-1.0 / 5040.0))))
    cos = 1.0 + sq * (-0.5 + sq * (1.0 / 24.0 + sq * (-1.0 / 720.0 + sq * (1.0 / 40320.0))))
    side = quarter.astype(I32) & 3
    odd = (side & 1) == 1
    real = jnp.where(odd, sin, cos)
    imag = jnp.where(odd, cos, sin)
    real = jnp.where((side == 1) | (side == 2), -real, real)
    imag = jnp.where(side >= 2, -imag, imag)
    return real, imag


def fine_kernel(nwave, pair_ref, fine_ref):
    devices = pair_ref.shape[1]
    nlon = fine_ref.shape[3]
    scale = 1.0 / math.sqrt(nlon)
    step_rows = 16
    lane = iota((step_rows, 128), 1).astype(F32)

    def block(i, carry):
        rows = pl.ds(pl.multiple_of(i * step_rows, step_rows), step_rows)
        for h in range(2):
            pair = pair_ref[0, rows, :].astype(F32)
            wave = pair if h == 0 else (nwave - 1.0) - pair
            wave = jnp.broadcast_to(wave, (step_rows, 128))
            c, s = turns(wave * lane, float(nlon))
            c, s = c * scale, s * scale
            rc, rs = turns(wave * 128.0, float(nlon))
            for t in range(nlon // 128):
                fine_ref[0, 2 * h, rows, t * 128 : (t + 1) * 128] = c.astype(BF16)
                fine_ref[0, 2 * h + 1, rows, t * 128 : (t + 1) * 128] = s.astype(BF16)
                c, s = c * rc - s * rs, s * rc + c * rs
        return carry

    lax.fori_loop(0, devices // step_rows, block, 0)


def coarse_kernel(nwave, pair_ref, coarse_ref):
    devices = pair_ref.shape[1]
    nlon = coarse_ref.shape[3] * 2
    scale = 1.0 / math.sqrt(nlon)
    step_rows = 16
    lane = iota((step_rows, 128), 1).astype(F32)
    lane_i = iota((step_rows, 128), 1)
    tail0 = ((lane_i // 32) * 160 + 128 + lane_i % 32).astype(F32)

    def block(i, carry):
        rows = pl.ds(pl.multiple_of(i * step_rows, step_rows), step_rows)
        for h in range(2):
            pair = pair_ref[0, rows, :].astype(F32)
            wave = pair if h == 0 else (nwave - 1.0) - pair
            wave = jnp.broadcast_to(wave, (step_rows, 128))
            amp, _ = turns(wave, 2.0 * nlon)
            amp = amp * (2.0 * scale)
            c, s = turns(wave * (4.0 * lane + 1.0), 2.0 * nlon)
            c, s = c * amp, s * amp
            rc, rs = turns(wave * 640.0, 2.0 * nlon)
            for t in range(8):
                coarse_ref[0, 2 * h, rows, t * 128 : (t + 1) * 128] = c.astype(BF16)
                coarse_ref[0, 2 * h + 1, rows, t * 128 : (t + 1) * 128] = s.astype(BF16)
                c, s = c * rc - s * rs, s * rc + c * rs
            c, s = turns(wave * (4.0 * tail0 + 1.0), 2.0 * nlon)
            c, s = c * amp, s * amp
            rc, rs = turns(wave * 2560.0, 2.0 * nlon)
            for t in range(8, 10):
                coarse_ref[0, 2 * h, rows, t * 128 : (t + 1) * 128] = c.astype(BF16)
                coarse_ref[0, 2 * h + 1, rows, t * 128 : (t + 1) * 128] = s.astype(BF16)
                c, s = c * rc - s * rs, s * rc + c * rs
        return carry

    lax.fori_loop(0, devices // step_rows, block, 0)


def table(kernel, pairs, nwave, width):
    group, devices, _ = pairs.shape
    size = group * 4 * devices * width
    return pl.pallas_call(
        functools.partial(kernel, nwave),
        grid=(group,),
        out_shape=pltpu.HBM((group, 4, devices, width), BF16),
        in_specs=[pl.BlockSpec((1, devices, 1), lambda s: (s, 0, 0))],
        out_specs=pl.BlockSpec((1, 4, devices, width), lambda s: (s, 0, 0, 0)),
        compiler_params=pltpu.CompilerParams(vmem_limit_bytes=8 * 2**20),
        cost_estimate=pl.CostEstimate(flops=10 * size, bytes_accessed=2 * size, transcendentals=0),
    )(pairs)


def fourier_kernel(piece_ref, fine_ref, out_ref, rows):
    blocks, group, lines, width = piece_ref.shape
    nlon = rows.shape[1]

    @pl.when(pl.program_id(0) == 0)
    def _():
        rows[...] = jnp.zeros_like(rows)
        for g in range(group):
            for j in range(blocks):
                rows[g * 128 : g * 128 + lines, j * width : (j + 1) * width] = piece_ref[j, g]

    out_ref[0] = lax.dot_general(
        fine_ref[0].reshape(out_ref.shape[1], nlon), rows[...], NT, preferred_element_type=F32
    )


def fourier(piece, fine):
    group, four, devices, nlon = fine.shape
    levels = piece.shape[1]
    return pl.pallas_call(
        fourier_kernel,
        grid=(group,),
        out_shape=jax.ShapeDtypeStruct((group, four * devices, levels * 128), F32),
        in_specs=[
            pl.BlockSpec(piece.shape, lambda s: (0, 0, 0, 0)),
            pl.BlockSpec((1, four, devices, nlon), lambda s: (s, 0, 0, 0)),
        ],
        out_specs=pl.BlockSpec((1, four * devices, levels * 128), lambda s: (s, 0, 0)),
        scratch_shapes=[pltpu.VMEM((levels * 128, nlon), BF16)],
        compiler_params=pltpu.CompilerParams(vmem_limit_bytes=16 * 2**20),
        name="fourier",
    )(piece, fine)


def unpack_kernel(came_ref, code_ref, out_ref, heat):
    blocks, groups = code_ref.shape[0], code_ref.shape[1]
    _, both, devices = came_ref.shape
    levels = 2
    cap = both // levels
    lines = heat.shape[1] // levels
    for j in range(blocks):

        def pick(g, carry):
            code = code_ref[j, g]
            owner = code // 128
            rank = code % 128
            marks = [
                (iota((devices, 128), 0) == owner[q : q + 1, :]).astype(F32).astype(BF16)
                for q in range(5)
            ]
            found = mm(came_ref[j], jnp.concatenate(marks, axis=1))
            for q in range(5):
                here = iota((cap, 128), 0) == rank[q : q + 1, :]
                for level in range(levels):
                    part = found[level * cap : (level + 1) * cap, q * 128 : (q + 1) * 128]
                    value = jnp.sum(jnp.where(here, part, 0.0), axis=0, keepdims=True)
                    if q < 4:
                        heat[j, pl.ds(level * lines + 4 * g + q, 1), :] = value
                    else:
                        tile = blocks + j // 4
                        mine = iota((1, 128), 1) // 32 == j % 4
                        for i in range(4):
                            moved = pltpu.roll(value, (32 * (j % 4 - i)) % 128, 1)
                            at = pl.ds(level * lines + 4 * g + i, 1)
                            heat[tile, at, :] = jnp.where(mine, moved, heat[tile, at, :])
            return carry

        lax.fori_loop(0, groups, pick, 0, unroll=2)
    for t in range(heat.shape[0]):
        out_ref[:, t * 128 : (t + 1) * 128] = heat[t].astype(BF16)


def unpack(came, code):
    blocks, groups = code.shape[0], code.shape[1]
    shape = (2 * groups * 4, blocks * 160)
    return pl.pallas_call(
        unpack_kernel,
        out_shape=jax.ShapeDtypeStruct(shape, BF16),
        scratch_shapes=[pltpu.VMEM((shape[1] // 128, shape[0], 128), F32)],
        compiler_params=pltpu.CompilerParams(vmem_limit_bytes=12 * 2**20),
        name="unpack",
    )(came, code)


def heated_kernel(nwave, heat_ref, coarse_ref, base_ref, pair_ref, sites_ref, out_ref, rows, mixed):
    step = pl.program_id(0)
    devices = pair_ref.shape[1]
    lines = heat_ref.shape[0] // 2
    cap = 80

    @pl.when(step == 0)
    def _():
        twice = iota((256, 2 * lines), 0)
        source = (twice // 128) * lines + (twice % 128) // 2
        keep = (source == iota((256, 2 * lines), 1)) & (twice % 128 < 2 * lines)
        rows[...] = mm(keep.astype(F32).astype(BF16), heat_ref[...]).astype(BF16)

    product = base_ref[0] + lax.dot_general(
        coarse_ref[0].reshape(4 * devices, rows.shape[1]),
        rows[...],
        NT,
        preferred_element_type=F32,
    )
    pair = pair_ref[0]
    for k in range(4):
        wave = pair if k < 2 else nwave - 1 - pair
        part = jnp.where(
            2 * wave < sites_ref[...], product[k * devices : (k + 1) * devices, :], 0.0
        )
        for level in range(2):
            mixed[pl.ds(level * 4 + k, devices, stride=8), :] = part[
                :, level * 128 : (level + 1) * 128
            ]
    for k in range(5):

        @pl.when(step == k)
        def _(k=k):
            out_ref[:, :, k * cap : (k + 1) * cap] = (
                mixed[...].reshape(devices, 8, 128)[:, :, :cap].astype(BF16)
            )


def heated(heat, coarse, base, pairs, sites, nwave):
    group, four, devices, half = coarse.shape
    return pl.pallas_call(
        functools.partial(heated_kernel, nwave),
        grid=(group,),
        out_shape=jax.ShapeDtypeStruct((devices, 8, group * 80), BF16),
        in_specs=[
            pl.BlockSpec(heat.shape, lambda s: (0, 0)),
            pl.BlockSpec((1, four, devices, half), lambda s: (s, 0, 0, 0)),
            pl.BlockSpec((1, four * devices, base.shape[2]), lambda s: (s, 0, 0)),
            pl.BlockSpec((1, devices, 1), lambda s: (s, 0, 0)),
            pl.BlockSpec(sites.shape, lambda s: (0, 0)),
        ],
        out_specs=pl.BlockSpec((devices, 8, group * 80), lambda s: (0, 0, 0)),
        scratch_shapes=[
            pltpu.VMEM((256, half), BF16),
            pltpu.VMEM((devices * 8, 128), F32),
        ],
        compiler_params=pltpu.CompilerParams(vmem_limit_bytes=16 * 2**20),
        name="heated",
    )(heat, coarse, base, pairs, sites)


def legendre_kernel(nwave, pair_ref, came_ref, basis_ref, out_ref, right):
    step = pl.program_id(0)
    ndeg, nlat = basis_ref.shape[1], basis_ref.shape[2]
    bands = nlat // 80
    for k in range(5):

        @pl.when(step == k)
        def _(k=k):
            for a in range(bands):
                block = came_ref[a * 8 : (a + 1) * 8, :, k * 80 : (k + 1) * 80].astype(F32)
                right[:, a * 80 : (a + 1) * 80] = block.reshape(64, 80).astype(BF16)

    pair = pair_ref[step]
    full = lax.dot_general(right[...], basis_ref[0], NT, preferred_element_type=F32)
    coeff = iota((64, ndeg), 1)
    head = (iota((64, ndeg), 0) % 4) < 2
    first = coeff < nwave - pair
    degree = jnp.where(first, pair + coeff, coeff - 1).astype(F32)
    factor = 1.0 / (1.0 + DIFFUSION * degree * (degree + 1.0) / (nwave * nwave))
    keep = (first & head) | (jnp.logical_not(first) & jnp.logical_not(head) & (coeff <= nwave))
    damped = jnp.where(keep, full * factor, 0.0).astype(BF16)
    synth = mm(damped, basis_ref[0])
    for k in range(5):

        @pl.when(step == k)
        def _(k=k):
            for a in range(bands):
                block = synth[:, a * 80 : (a + 1) * 80].reshape(8, 8, 80)
                out_ref[a * 8 : (a + 1) * 8, :, k * 80 : (k + 1) * 80] = block.astype(BF16)


def legendre(pairs, came, basis, nwave):
    group, ndeg, nlat = basis.shape
    return pl.pallas_call(
        functools.partial(legendre_kernel, nwave),
        grid_spec=pltpu.PrefetchScalarGridSpec(
            num_scalar_prefetch=1,
            grid=(group,),
            in_specs=[
                pl.BlockSpec(came.shape, lambda s, p: (0, 0, 0)),
                pl.BlockSpec((1, ndeg, nlat), lambda s, p: (s, 0, 0)),
            ],
            out_specs=pl.BlockSpec(came.shape, lambda s, p: (0, 0, 0)),
            scratch_shapes=[pltpu.VMEM((64, nlat), BF16)],
        ),
        out_shape=jax.ShapeDtypeStruct(came.shape, BF16),
        compiler_params=pltpu.CompilerParams(vmem_limit_bytes=24 * 2**20),
        name="legendre",
    )(pairs, came, basis)


def inverse_kernel(came_ref, fine_ref, out_ref, mixed, left, total):
    step = pl.program_id(0)
    devices = came_ref.shape[0]
    blocks, _, width = out_ref.shape
    for k in range(5):

        @pl.when(step == k)
        def _(k=k):
            mixed[:, :80] = (
                came_ref[:, :, k * 80 : (k + 1) * 80].astype(F32).reshape(devices * 8, 80)
            )

    for k in range(4):
        for level in range(2):
            part = mixed[pl.ds(level * 4 + k, devices, stride=8), :]
            left[level * 80 : (level + 1) * 80, k * devices : (k + 1) * devices] = part.T[
                :80, :
            ].astype(BF16)
    product = mm(left[...], fine_ref[0].reshape(4 * devices, total.shape[1]))

    @pl.when(step == 0)
    def _():
        total[...] = product

    @pl.when(step > 0)
    def _():
        total[...] += product

    @pl.when(step == pl.num_programs(0) - 1)
    def _():
        for j in range(blocks):
            out_ref[j] = total[:, j * width : (j + 1) * width].astype(BF16)


def inverse(came, fine, blocks):
    group, four, devices, nlon = fine.shape
    return pl.pallas_call(
        inverse_kernel,
        grid=(group,),
        out_shape=jax.ShapeDtypeStruct((blocks, 160, nlon // blocks), BF16),
        in_specs=[
            pl.BlockSpec(came.shape, lambda s: (0, 0, 0)),
            pl.BlockSpec((1, four, devices, nlon), lambda s: (s, 0, 0, 0)),
        ],
        out_specs=pl.BlockSpec((blocks, 160, nlon // blocks), lambda s: (0, 0, 0)),
        scratch_shapes=[
            pltpu.VMEM((devices * 8, 128), F32),
            pltpu.VMEM((160, four * devices), BF16),
            pltpu.VMEM((160, nlon), F32),
        ],
        compiler_params=pltpu.CompilerParams(vmem_limit_bytes=24 * 2**20),
        name="inverse",
    )(came, fine)


def in_hbm(x):
    return pltpu.with_memory_space_constraint(x, pltpu.HBM)


def swap(x, axes):
    return lax.all_to_all(x, axes, split_axis=0, concat_axis=0, tiled=True)


def per_device(state, holder, depths, pairs, sites, basis):
    levels, lines, width = state.shape
    group, _, _ = basis.shape
    nwave = pairs.shape[0] * 2
    nlon = nwave * 2
    lat_size = lax.axis_size("lat")
    lon_size = lax.axis_size("lon")
    devices = lat_size * lon_size
    level_group = levels // lon_size
    rows, cols = lines // 2, width // 2
    me = lax.axis_index("lat") * lon_size + lax.axis_index("lon")
    slots = pairs.reshape(devices, group).T[:, :, None]
    limits = jnp.pad(sites, (0, 128 - lines))
    limits = jnp.concatenate([limits, limits])[None, :]
    owner = jnp.pad(holder.reshape(rows, cols), ((0, 0), (0, 256 - cols)), constant_values=-1)

    piece = swap(state.astype(BF16), "lon").reshape(lon_size, level_group, lines, width)

    sorted_cols, code = pack(state, owner)
    outgoing = sorted_cols.reshape(5, devices, levels, 16).transpose(1, 2, 0, 3)
    came = swap(outgoing.reshape(devices, levels, 80), ALL)
    codes = swap(jnp.broadcast_to(code[None], (lon_size,) + code.shape), "lon")
    fine = table(fine_kernel, slots, nwave, nlon)
    heat = radiate(came, in_hbm(depths[0]), lat_size, lon_size)
    returned = swap(heat, ALL)
    coarse = table(coarse_kernel, slots, nwave, nlon // 2)
    base = fourier(piece, in_hbm(fine))
    returned = returned.reshape(devices, level_group, lon_size, 80).transpose(2, 1, 3, 0)
    warm = unpack(returned.reshape(lon_size, level_group * 80, devices), codes)
    sending = heated(warm, in_hbm(coarse), base, slots, limits, nwave)
    arrived = swap(sending, ALL)
    mine = lax.dynamic_slice_in_dim(pairs, me * group, group)
    spread = legendre(mine, arrived, in_hbm(basis.transpose(0, 2, 1)), nwave)
    back = swap(spread, ALL)
    grid = inverse(back, in_hbm(fine), lon_size)
    grid = swap(grid, "lon")
    return grid.reshape(levels, lines, width).astype(F32)


def solution(mesh):
    in_specs = (
        P(None, "lat", "lon"),
        P(("lat", "lon"), None, None),
        P(("lat", "lon"), None, None, None),
        P(),
        P("lat"),
        P(("lat", "lon"), None, None),
    )
    out_specs = P(None, "lat", "lon")
    return jax.shard_map(
        per_device, mesh=mesh, in_specs=in_specs, out_specs=out_specs, check_vma=False
    )
```

```python
import functools
import math

import jax
import jax.numpy as jnp
from jax import lax
from jax.experimental import pallas as pl
from jax.experimental.pallas import tpu as pltpu
from jax.sharding import PartitionSpec as P


DIFFUSION = 4.0
BF16 = jnp.bfloat16
F32 = jnp.float32
I32 = jnp.int32
ALL = ("lat", "lon")
NT = (((1,), (1,)), ((), ()))


def iota(shape, dim):
    return lax.broadcasted_iota(I32, shape, dim)


def mm(a, b):
    return jnp.dot(a, b, preferred_element_type=F32)


def split_mm_right(x, b):
    hi = x.astype(BF16)
    lo = (x - hi.astype(F32)).astype(BF16)
    return mm(hi, b) + mm(lo, b)


def pack_kernel(state_ref, owner_ref, out_ref, code_ref, halves, coarse, marks, owners, values, total):
    levels, lines, width = state_ref.shape
    rows, lanes = owner_ref.shape
    devices = 128
    low = 16
    high = out_ref.shape[0] // devices
    pool_x = (iota((width, lanes), 0) // 2 == iota((width, lanes), 1)).astype(F32).astype(BF16)
    summed = split_mm_right(state_ref[...].reshape(levels * lines, width), pool_x)
    for t in range(2):
        halves[t] = summed[:, t * 128 : (t + 1) * 128]
    for level in range(levels):
        for t in range(2):
            even = halves[t, pl.ds(level * lines, rows, stride=2), :]
            odd = halves[t, pl.ds(level * lines + 1, rows, stride=2), :]
            mean = 0.25 * (even + odd)
            coarse[level, :, t * 128 : (t + 1) * 128] = mean.astype(BF16).astype(F32)
    before = (iota((lanes, lanes), 0) < iota((lanes, lanes), 1)).astype(F32).astype(BF16)
    total[...] = jnp.zeros_like(total)
    short = iota((8, 128), 1) < 32

    def tails(x):
        moved = x
        for i in range(1, 4):
            moved = jnp.where(iota((8, 128), 0) % 4 == i, pltpu.roll(x, 32 * i, 1), moved)
        return [jnp.sum(moved[4 * i : 4 * i + 4, :], axis=0, keepdims=True) for i in range(2)]

    def chunk(c, base):
        start = pl.multiple_of(c * 8, 8)
        owner8 = owner_ref[pl.ds(start, 8), :]
        for u in range(8):
            match = (iota((devices, lanes), 0) == owner8[u : u + 1, :]).astype(F32)
            marks[u * devices : (u + 1) * devices, :] = match.astype(BF16)
        counted = mm(marks[...], before)
        ranks = []
        for u in range(8):
            here = counted[u * devices : (u + 1) * devices, :]
            match = (iota((devices, lanes), 0) == owner8[u : u + 1, :]).astype(F32)
            both = jnp.concatenate([base, base], axis=1)
            ranks.append(jnp.sum(match * (here + both), axis=0, keepdims=True))
            base = base + here[:, lanes - 1 : lanes]
        code = owner8 * 128 + jnp.concatenate(ranks, axis=0).astype(I32)
        ends = tails(jnp.where(short, code[:, 128:], 0))
        for i in range(2):
            code_ref[2 * c + i] = jnp.concatenate(
                [code[4 * i : 4 * i + 4, :128], ends[i], jnp.zeros((3, 128), I32)], axis=0
            )
        lines8 = [code[u : u + 1, :128] for u in range(8)] + ends
        temps = []
        for level in range(levels):
            block = coarse[level, pl.ds(start, 8), :]
            temps.append([block[u : u + 1, :128] for u in range(8)] + tails(block[:, 128:]))
        for u in range(10):
            span = slice(u * 128, (u + 1) * 128)
            owner = lines8[u] // 128
            rank = lines8[u] % 128
            match = (iota((devices, 128), 0) == owner).astype(F32)
            for h in range(high):
                part = ((rank // low) == h).astype(F32)
                owners[h * devices : (h + 1) * devices, span] = (match * part).astype(BF16)
            slot = (iota((low, 128), 0) == rank % low).astype(F32)
            for level in range(levels):
                values[level * low : (level + 1) * low, span] = (
                    slot * temps[level][u]
                ).astype(BF16)
        total[...] += lax.dot_general(
            owners[...], values[...], NT, preferred_element_type=F32
        )
        return base

    lax.fori_loop(0, rows // 8, chunk, jnp.zeros((devices, devices), F32))
    out_ref[...] = total[...].astype(BF16)


def pack(state, owner):
    levels, lines, _ = state.shape
    rows, lanes = owner.shape
    return pl.pallas_call(
        pack_kernel,
        out_shape=(
            jax.ShapeDtypeStruct((640, levels * 16), BF16),
            jax.ShapeDtypeStruct((rows // 4, 8, 128), I32),
        ),
        scratch_shapes=[
            pltpu.VMEM((2, levels * lines, 128), F32),
            pltpu.VMEM((levels, rows, lanes), F32),
            pltpu.VMEM((8 * 128, lanes), BF16),
            pltpu.VMEM((640, 1280), BF16),
            pltpu.VMEM((levels * 16, 1280), BF16),
            pltpu.VMEM((640, levels * 16), F32),
        ],
        compiler_params=pltpu.CompilerParams(vmem_limit_bytes=20 * 2**20),
        cost_estimate=pl.CostEstimate(flops=6 * 10**9, bytes_accessed=2 * 10**6, transcendentals=0),
        name="pack",
    )(state, owner)


def radiate_kernel(came_ref, depth_ref, out_ref, temp, lost, down, heat):
    blocks, levels, cap = came_ref.shape
    bands = depth_ref.shape[1]
    for j in range(blocks):
        temp[:, j * cap : (j + 1) * cap] = came_ref[j].astype(F32)
    temp[...] = jnp.exp(0.5 * temp[...])
    weight = (iota((bands, 1), 0).astype(F32) + 1.0) * (2.0 / (bands * (bands + 1)))
    flux = jnp.zeros((bands, blocks * cap), F32)
    for level in range(levels):
        share = 1.0 - jnp.exp(-depth_ref[level].astype(F32))
        lost[level] = share
        step = share * (flux - temp[level : level + 1, :])
        down[level] = step
        flux = flux - step
    flux = jnp.broadcast_to(temp[levels - 1 : levels, :], flux.shape)
    for level in reversed(range(levels)):
        step = lost[level] * (flux - temp[level : level + 1, :])
        flux = flux - step
        heat[level : level + 1, :] = jnp.sum(
            (step + down[level]) * weight, axis=0, keepdims=True
        )
    group = out_ref.shape[1]
    for b in range(levels // group):
        out_ref[b] = heat[b * group : (b + 1) * group, :].astype(BF16)


def radiate(came, depth, lat_size, lon_size):
    devices, levels, cap = came.shape
    bands = depth.shape[1]
    width = lon_size * cap
    group = levels // lon_size
    return pl.pallas_call(
        radiate_kernel,
        grid=(lat_size,),
        out_shape=jax.ShapeDtypeStruct((devices, group, width), BF16),
        in_specs=[
            pl.BlockSpec((lon_size, levels, cap), lambda a: (a, 0, 0)),
            pl.BlockSpec((levels, bands, width), lambda a: (0, 0, a)),
        ],
        out_specs=pl.BlockSpec((lon_size, group, width), lambda a: (a, 0, 0)),
        scratch_shapes=[
            pltpu.VMEM((levels, width), F32),
            pltpu.VMEM((levels, bands, width), F32),
            pltpu.VMEM((levels, bands, width), F32),
            pltpu.VMEM((levels, width), F32),
        ],
        compiler_params=pltpu.CompilerParams(vmem_limit_bytes=16 * 2**20),
        name="radiate",
    )(came, depth)


def turns(count, whole):
    quarter = jnp.floor(count * (4.0 / whole) + 0.5)
    angle = (count - quarter * (whole / 4.0)) * (2.0 * math.pi / whole)
    sq = angle * angle
    sin = angle * (1.0 + sq * (-1.0 / 6.0 + sq * (1.0 / 120.0 + sq * (-1.0 / 5040.0))))
    cos = 1.0 + sq * (-0.5 + sq * (1.0 / 24.0 + sq * (-1.0 / 720.0 + sq * (1.0 / 40320.0))))
    side = quarter.astype(I32) & 3
    odd = (side & 1) == 1
    real = jnp.where(odd, sin, cos)
    imag = jnp.where(odd, cos, sin)
    real = jnp.where((side == 1) | (side == 2), -real, real)
    imag = jnp.where(side >= 2, -imag, imag)
    return real, imag


def turned(c, s, rc, rs):
    return c * rc - s * rs, s * rc + c * rs


def fine_kernel(nwave, pair_ref, fine_ref):
    devices = pair_ref.shape[1]
    nlon = fine_ref.shape[3]
    scale = 1.0 / math.sqrt(nlon)
    step_rows = 16
    lane = iota((step_rows, 128), 1)

    def block(i, carry):
        rows = pl.ds(pl.multiple_of(i * step_rows, step_rows), step_rows)
        for h in range(2):
            pair = pair_ref[0, rows, :].astype(F32)
            wave = pair if h == 0 else (nwave - 1.0) - pair
            wave = jnp.broadcast_to(wave, (step_rows, 128))

            def put(t, c, s):
                fine_ref[0, 2 * h, rows, t * 128 : (t + 1) * 128] = c.astype(BF16)
                fine_ref[0, 2 * h + 1, rows, t * 128 : (t + 1) * 128] = s.astype(BF16)

            c, s = turns(wave * lane.astype(F32), float(nlon))
            c, s = c * scale, s * scale
            r64 = turns(wave * 64.0, float(nlon))
            r128 = turned(*r64, *r64)
            r256 = turned(*r128, *r128)
            r320 = turned(*r256, *r64)
            r512 = turned(*r256, *r256)
            r640 = turned(*r320, *r320)
            low = lane < 64
            last = turned(
                c, s, jnp.where(low, r256[0], r512[0]), jnp.where(low, r256[1], r512[1])
            )
            for t in range(16, 20):
                put(t, *last)
                last = turned(*last, *r640)
            for j in range(8):
                put(2 * j, c, s)
                put(2 * j + 1, *turned(c, s, *r128))
                c, s = turned(c, s, *r320)
        return carry

    lax.fori_loop(0, devices // step_rows, block, 0)


def table(kernel, pairs, nwave, width):
    group, devices, _ = pairs.shape
    size = group * 4 * devices * width
    return pl.pallas_call(
        functools.partial(kernel, nwave),
        grid=(group,),
        out_shape=pltpu.HBM((group, 4, devices, width), BF16),
        in_specs=[pl.BlockSpec((1, devices, 1), lambda s: (s, 0, 0))],
        out_specs=pl.BlockSpec((1, 4, devices, width), lambda s: (s, 0, 0, 0)),
        compiler_params=pltpu.CompilerParams(vmem_limit_bytes=8 * 2**20),
        cost_estimate=pl.CostEstimate(flops=10 * size, bytes_accessed=2 * size, transcendentals=0),
    )(pairs)


def lay_kernel(state_ref, code_ref, out_ref, codes):
    blocks = out_ref.shape[0]
    groups = code_ref.shape[0]
    lines = state_ref.shape[1]
    codes[...] = jnp.zeros_like(codes)
    for g in range(groups):
        code = code_ref[g, :5, :]
        codes[5 * g : 5 * g + 5, :] = (code // 128).astype(F32)
        codes[5 * (groups + g) : 5 * (groups + g) + 5, :] = (code % 128).astype(F32)
    packed = codes[...].astype(BF16)
    for b in range(blocks):
        for level in range(2):
            here = state_ref[2 * b + level].astype(BF16)
            for t in range(2):
                first = (2 * t + level) * lines
                out_ref[b, first : first + lines, :] = here[:, t * 128 : (t + 1) * 128]
            out_ref[b, 4 * lines : 5 * lines, level * 64 : (level + 1) * 64] = here[:, 256:320]
        out_ref[b, 5 * lines :, :] = packed


def lay(state, code, blocks):
    lines = state.shape[1]
    return pl.pallas_call(
        lay_kernel,
        out_shape=jax.ShapeDtypeStruct((blocks, 5 * lines + 104, 128), BF16),
        scratch_shapes=[pltpu.VMEM((104, 128), F32)],
        compiler_params=pltpu.CompilerParams(vmem_limit_bytes=12 * 2**20),
        cost_estimate=pl.CostEstimate(flops=10**6, bytes_accessed=4 * 10**6, transcendentals=0),
        name="lay",
    )(state, code)


def unpack_kernel(came_ref, moved_ref, out_ref, heat):
    blocks, both, devices = came_ref.shape
    levels = 2
    groups = 10
    cap = both // levels
    lines = heat.shape[1] // levels
    first = 400
    own = iota((devices, 128), 0).astype(F32)
    place = iota((cap, 128), 0).astype(F32)

    def block(j, carry):
        table = came_ref[j]
        for g in range(groups):
            marks, ranks = [], []
            for q in range(5):
                row = first + 5 * g + q
                owner = moved_ref[j, row : row + 1, :].astype(F32)
                row += 5 * groups
                ranks.append(moved_ref[j, row : row + 1, :].astype(F32))
                marks.append((own == owner).astype(F32).astype(BF16))
            found = mm(table, jnp.concatenate(marks, axis=1))
            for q in range(5):
                here = place == ranks[q]
                for level in range(levels):
                    part = found[level * cap : (level + 1) * cap, q * 128 : (q + 1) * 128]
                    value = jnp.sum(jnp.where(here, part, 0.0), axis=0, keepdims=True)
                    line = level * lines + 4 * g
                    if q < 4:
                        heat[j, line + q : line + q + 1, :] = value
                    else:
                        tile = blocks + j // 4
                        mine = iota((1, 128), 1) // 32 == j % 4
                        for i in range(4):
                            moved = pltpu.roll(value, (32 * (j % 4 - i) + 128) % 128, 1)
                            old = heat[tile, line + i : line + i + 1, :]
                            heat[tile, line + i : line + i + 1, :] = jnp.where(mine, moved, old)
        return carry

    lax.fori_loop(0, blocks, block, 0)
    for t in range(heat.shape[0]):
        out_ref[:, t * 128 : (t + 1) * 128] = heat[t].astype(BF16)


def unpack(came, moved):
    blocks = came.shape[0]
    shape = (80, blocks * 160)
    return pl.pallas_call(
        unpack_kernel,
        out_shape=jax.ShapeDtypeStruct(shape, BF16),
        scratch_shapes=[pltpu.VMEM((shape[1] // 128, shape[0], 128), F32)],
        compiler_params=pltpu.CompilerParams(vmem_limit_bytes=12 * 2**20),
        name="unpack",
    )(came, moved)


def forward_kernel(nwave, heat_ref, moved_ref, fine_ref, pair_ref, sites_ref, out_ref, rows, mixed):
    step = pl.program_id(0)
    devices = pair_ref.shape[1]
    lines = heat_ref.shape[0]
    cap = lines

    @pl.when(step == 0)
    def _():
        rows[...] = jnp.zeros_like(rows)
        place = iota((256, lines), 0)
        source = (place // 128) * (lines // 2) + (place % 128) // 2
        twice = (source == iota((256, lines), 1)) & (place % 128 < lines)
        double = mm(twice.astype(F32).astype(BF16), heat_ref[...]).astype(BF16)
        wide = (iota((128, 256), 1) // 2 == iota((128, 256), 0)).astype(F32).astype(BF16)
        for t in range(10):
            warm = mm(double[:, t * 128 : (t + 1) * 128], wide)
            for level in range(2):
                here = warm[level * 128 : level * 128 + lines, :]
                at = slice(level * 128, level * 128 + lines)
                if t < 8:
                    for h in range(2):
                        first = (2 * h + level) * lines
                        cold = moved_ref[t, first : first + lines, :].astype(F32)
                        span = slice(t * 256 + h * 128, t * 256 + (h + 1) * 128)
                        rows[at, span] = (cold + here[:, h * 128 : (h + 1) * 128]).astype(BF16)
                else:
                    cold = jnp.concatenate(
                        [
                            moved_ref[
                                4 * (t - 8) + q,
                                4 * lines : 5 * lines,
                                level * 64 : (level + 1) * 64,
                            ].astype(F32)
                            for q in range(4)
                        ],
                        axis=1,
                    )
                    rows[at, t * 256 : (t + 1) * 256] = (cold + here).astype(BF16)

    product = lax.dot_general(
        fine_ref[0].reshape(4 * devices, rows.shape[1]),
        rows[...],
        NT,
        preferred_element_type=F32,
    )
    pair = pair_ref[0]
    for k in range(4):
        wave = pair if k < 2 else nwave - 1 - pair
        part = jnp.where(
            2 * wave < sites_ref[...], product[k * devices : (k + 1) * devices, :], 0.0
        )
        for level in range(2):
            mixed[pl.ds(level * 4 + k, devices, stride=8), :] = part[
                :, level * 128 : (level + 1) * 128
            ]
    for k in range(5):

        @pl.when(step == k)
        def _(k=k):
            out_ref[:, :, k * cap : (k + 1) * cap] = (
                mixed[...].reshape(devices, 8, 128)[:, :, :cap].astype(BF16)
            )


def forward(heat, moved, fine, pairs, sites, nwave):
    group, four, devices, nlon = fine.shape
    return pl.pallas_call(
        functools.partial(forward_kernel, nwave),
        grid=(group,),
        out_shape=jax.ShapeDtypeStruct((devices, 8, group * 80), BF16),
        in_specs=[
            pl.BlockSpec(heat.shape, lambda s: (0, 0)),
            pl.BlockSpec(moved.shape, lambda s: (0, 0, 0)),
            pl.BlockSpec((1, four, devices, nlon), lambda s: (s, 0, 0, 0)),
            pl.BlockSpec((1, devices, 1), lambda s: (s, 0, 0)),
            pl.BlockSpec(sites.shape, lambda s: (0, 0)),
        ],
        out_specs=pl.BlockSpec((devices, 8, group * 80), lambda s: (0, 0, 0)),
        scratch_shapes=[
            pltpu.VMEM((256, nlon), BF16),
            pltpu.VMEM((devices * 8, 128), F32),
        ],
        compiler_params=pltpu.CompilerParams(vmem_limit_bytes=20 * 2**20),
        name="forward",
    )(heat, moved, fine, pairs, sites)


def legendre_kernel(nwave, pair_ref, came_ref, basis_ref, out_ref, right):
    step = pl.program_id(0)
    ndeg, nlat = basis_ref.shape[1], basis_ref.shape[2]
    bands = nlat // 80
    for k in range(5):

        @pl.when(step == k)
        def _(k=k):
            for a in range(bands):
                block = came_ref[a * 8 : (a + 1) * 8, :, k * 80 : (k + 1) * 80].astype(F32)
                right[:, a * 80 : (a + 1) * 80] = block.reshape(64, 80).astype(BF16)

    pair = pair_ref[step]
    full = lax.dot_general(right[...], basis_ref[0], NT, preferred_element_type=F32)
    coeff = iota((64, ndeg), 1)
    head = (iota((64, ndeg), 0) % 4) < 2
    first = coeff < nwave - pair
    degree = jnp.where(first, pair + coeff, coeff - 1).astype(F32)
    factor = 1.0 / (1.0 + DIFFUSION * degree * (degree + 1.0) / (nwave * nwave))
    keep = (first & head) | (jnp.logical_not(first) & jnp.logical_not(head) & (coeff <= nwave))
    damped = jnp.where(keep, full * factor, 0.0).astype(BF16)
    synth = mm(damped, basis_ref[0])
    for k in range(5):

        @pl.when(step == k)
        def _(k=k):
            for a in range(bands):
                block = synth[:, a * 80 : (a + 1) * 80].reshape(8, 8, 80)
                out_ref[a * 8 : (a + 1) * 8, :, k * 80 : (k + 1) * 80] = block.astype(BF16)


def legendre(pairs, came, basis, nwave):
    group, ndeg, nlat = basis.shape
    return pl.pallas_call(
        functools.partial(legendre_kernel, nwave),
        grid_spec=pltpu.PrefetchScalarGridSpec(
            num_scalar_prefetch=1,
            grid=(group,),
            in_specs=[
                pl.BlockSpec(came.shape, lambda s, p: (0, 0, 0)),
                pl.BlockSpec((1, ndeg, nlat), lambda s, p: (s, 0, 0)),
            ],
            out_specs=pl.BlockSpec(came.shape, lambda s, p: (0, 0, 0)),
            scratch_shapes=[pltpu.VMEM((64, nlat), BF16)],
        ),
        out_shape=jax.ShapeDtypeStruct(came.shape, BF16),
        compiler_params=pltpu.CompilerParams(vmem_limit_bytes=24 * 2**20),
        name="legendre",
    )(pairs, came, basis)


def inverse_kernel(came_ref, fine_ref, out_ref, mixed, left, total):
    step = pl.program_id(0)
    devices = came_ref.shape[0]
    blocks, _, _ = out_ref.shape
    for k in range(5):

        @pl.when(step == k)
        def _(k=k):
            mixed[:, :80] = (
                came_ref[:, :, k * 80 : (k + 1) * 80].astype(F32).reshape(devices * 8, 80)
            )

    for k in range(4):
        for level in range(2):
            part = mixed[pl.ds(level * 4 + k, devices, stride=8), :]
            left[level * 80 : (level + 1) * 80, k * devices : (k + 1) * devices] = part.T[
                :80, :
            ].astype(BF16)
    product = mm(left[...], fine_ref[0].reshape(4 * devices, total.shape[1]))

    @pl.when(step == 0)
    def _():
        total[...] = product

    @pl.when(step > 0)
    def _():
        total[...] += product

    @pl.when(step == pl.num_programs(0) - 1)
    def _():
        for j in range(blocks):
            out_ref[j, :, :256] = total[:, j * 256 : (j + 1) * 256].astype(BF16)
            first = blocks * 256 + j * 64
            out_ref[j, :, 256:] = total[:, first : first + 64].astype(BF16)


def inverse(came, fine, blocks):
    group, four, devices, nlon = fine.shape
    return pl.pallas_call(
        inverse_kernel,
        grid=(group,),
        out_shape=jax.ShapeDtypeStruct((blocks, 160, nlon // blocks), BF16),
        in_specs=[
            pl.BlockSpec(came.shape, lambda s: (0, 0, 0)),
            pl.BlockSpec((1, four, devices, nlon), lambda s: (s, 0, 0, 0)),
        ],
        out_specs=pl.BlockSpec((blocks, 160, nlon // blocks), lambda s: (0, 0, 0)),
        scratch_shapes=[
            pltpu.VMEM((devices * 8, 128), F32),
            pltpu.VMEM((160, four * devices), BF16),
            pltpu.VMEM((160, nlon), F32),
        ],
        compiler_params=pltpu.CompilerParams(vmem_limit_bytes=24 * 2**20),
        name="inverse",
    )(came, fine)


def in_hbm(x):
    return pltpu.with_memory_space_constraint(x, pltpu.HBM)


def swap(x, axes):
    return lax.all_to_all(x, axes, split_axis=0, concat_axis=0, tiled=True)


def per_device(state, holder, depths, pairs, sites, basis):
    levels, lines, width = state.shape
    group, _, _ = basis.shape
    nwave = pairs.shape[0] * 2
    nlon = nwave * 2
    lat_size = lax.axis_size("lat")
    lon_size = lax.axis_size("lon")
    devices = lat_size * lon_size
    level_group = levels // lon_size
    rows, cols = lines // 2, width // 2
    me = lax.axis_index("lat") * lon_size + lax.axis_index("lon")
    slots = pairs.reshape(devices, group).T[:, :, None]
    limits = jnp.pad(sites, (0, 128 - lines))
    limits = jnp.concatenate([limits, limits])[None, :]
    owner = jnp.pad(holder.reshape(rows, cols), ((0, 0), (0, 256 - cols)), constant_values=-1)

    sorted_cols, code = pack(state, owner)
    outgoing = sorted_cols.reshape(5, devices, levels, 16).transpose(1, 2, 0, 3)
    came = swap(outgoing.reshape(devices, levels, 80), ALL)
    fine = table(fine_kernel, slots, nwave, nlon)
    laid = lay(state, code, lon_size)
    moved = swap(laid, "lon")
    heat = radiate(came, in_hbm(depths[0]), lat_size, lon_size)
    returned = swap(heat, ALL)
    returned = returned.reshape(devices, level_group, lon_size, 80).transpose(2, 1, 3, 0)
    warm = unpack(returned.reshape(lon_size, level_group * 80, devices), moved)
    sending = forward(warm, moved, in_hbm(fine), slots, limits, nwave)
    arrived = swap(sending, ALL)
    mine = lax.dynamic_slice_in_dim(pairs, me * group, group)
    spread = legendre(mine, arrived, in_hbm(basis.transpose(0, 2, 1)), nwave)
    back = swap(spread, ALL)
    grid = inverse(back, in_hbm(fine), lon_size)
    grid = swap(grid, "lon")
    return grid.reshape(levels, lines, width).astype(F32)


def solution(mesh):
    in_specs = (
        P(None, "lat", "lon"),
        P(("lat", "lon"), None, None),
        P(("lat", "lon"), None, None, None),
        P(),
        P("lat"),
        P(("lat", "lon"), None, None),
    )
    out_specs = P(None, "lat", "lon")
    return jax.shard_map(
        per_device, mesh=mesh, in_specs=in_specs, out_specs=out_specs, check_vma=False
    )
```

```python
import functools
import math

import jax
import jax.numpy as jnp
from jax import lax
from jax.experimental import pallas as pl
from jax.experimental.pallas import tpu as pltpu
from jax.sharding import PartitionSpec as P


DIFFUSION = 4.0
BF16 = jnp.bfloat16
F32 = jnp.float32
I32 = jnp.int32
ALL = ("lat", "lon")
NT = (((1,), (1,)), ((), ()))


def iota(shape, dim):
    return lax.broadcasted_iota(I32, shape, dim)


def mm(a, b):
    return jnp.dot(a, b, preferred_element_type=F32)


def split_mm_right(x, b):
    hi = x.astype(BF16)
    lo = (x - hi.astype(F32)).astype(BF16)
    return mm(hi, b) + mm(lo, b)


def pack_kernel(
    state_ref, owner_ref, out_ref, code_ref, state, halves, coarse, marks, owners, values, total, sem
):
    levels, lines, width = state_ref.shape
    rows, lanes = owner_ref.shape
    devices = 128
    low = 16
    high = out_ref.shape[0] // devices
    fetch = pltpu.make_async_copy(state_ref, state, sem)
    fetch.start()
    pool_x = (iota((width, lanes), 0) // 2 == iota((width, lanes), 1)).astype(F32).astype(BF16)
    before = (iota((lanes, lanes), 0) < iota((lanes, lanes), 1)).astype(F32).astype(BF16)
    total[...] = jnp.zeros_like(total)
    short = iota((8, 128), 1) < 32

    def tails(x):
        moved = x
        for i in range(1, 4):
            moved = jnp.where(iota((8, 128), 0) % 4 == i, pltpu.roll(x, 32 * i, 1), moved)
        return [jnp.sum(moved[4 * i : 4 * i + 4, :], axis=0, keepdims=True) for i in range(2)]

    def chunk(c, base):
        start = pl.multiple_of(c * 8, 8)
        owner8 = owner_ref[pl.ds(start, 8), :]
        for u in range(8):
            match = (iota((devices, lanes), 0) == owner8[u : u + 1, :]).astype(F32)
            marks[u * devices : (u + 1) * devices, :] = match.astype(BF16)
        counted = mm(marks[...], before)
        ranks = []
        for u in range(8):
            here = counted[u * devices : (u + 1) * devices, :]
            match = (iota((devices, lanes), 0) == owner8[u : u + 1, :]).astype(F32)
            both = jnp.concatenate([base, base], axis=1)
            ranks.append(jnp.sum(match * (here + both), axis=0, keepdims=True))
            base = base + here[:, lanes - 1 : lanes]
        code = owner8 * 128 + jnp.concatenate(ranks, axis=0).astype(I32)
        ends = tails(jnp.where(short, code[:, 128:], 0))
        for i in range(2):
            code_ref[2 * c + i] = jnp.concatenate(
                [code[4 * i : 4 * i + 4, :128], ends[i], jnp.zeros((3, 128), I32)], axis=0
            )
        return base

    def sort(c, carry):
        start = pl.multiple_of(c * 8, 8)
        codes = [code_ref[2 * c + i] for i in range(2)]
        temps = []
        for level in range(levels):
            block = coarse[level, pl.ds(start, 8), :]
            ends = tails(block[:, 128:])
            temps.append(
                [block[4 * i + u : 4 * i + u + 1, :128] if u < 4 else ends[i] for i in range(2) for u in range(5)]
            )
        for u in range(10):
            span = slice(u * 128, (u + 1) * 128)
            code = codes[u // 5][u % 5 : u % 5 + 1, :]
            owner = code // 128
            rank = code % 128
            match = (iota((devices, 128), 0) == owner).astype(F32)
            for h in range(high):
                part = ((rank // low) == h).astype(F32)
                owners[h * devices : (h + 1) * devices, span] = (match * part).astype(BF16)
            slot = (iota((low, 128), 0) == rank % low).astype(F32)
            for level in range(levels):
                values[level * low : (level + 1) * low, span] = (
                    slot * temps[level][u]
                ).astype(BF16)
        total[...] += lax.dot_general(
            owners[...], values[...], NT, preferred_element_type=F32
        )
        return carry

    lax.fori_loop(0, rows // 8, chunk, jnp.zeros((devices, devices), F32))
    fetch.wait()
    summed = split_mm_right(state[...].reshape(levels * lines, width), pool_x)
    for t in range(2):
        halves[t] = summed[:, t * 128 : (t + 1) * 128]
    for level in range(levels):
        for t in range(2):
            even = halves[t, pl.ds(level * lines, rows, stride=2), :]
            odd = halves[t, pl.ds(level * lines + 1, rows, stride=2), :]
            mean = 0.25 * (even + odd)
            coarse[level, :, t * 128 : (t + 1) * 128] = mean.astype(BF16).astype(F32)
    lax.fori_loop(0, rows // 8, sort, 0)
    out_ref[...] = total[...].astype(BF16)


def pack(state, owner):
    levels, lines, _ = state.shape
    rows, lanes = owner.shape
    return pl.pallas_call(
        pack_kernel,
        out_shape=(
            jax.ShapeDtypeStruct((640, levels * 16), BF16),
            jax.ShapeDtypeStruct((rows // 4, 8, 128), I32),
        ),
        in_specs=[
            pl.BlockSpec(memory_space=pltpu.HBM),
            pl.BlockSpec(memory_space=pltpu.VMEM),
        ],
        scratch_shapes=[
            pltpu.VMEM(state.shape, F32),
            pltpu.VMEM((2, levels * lines, 128), F32),
            pltpu.VMEM((levels, rows, lanes), F32),
            pltpu.VMEM((8 * 128, lanes), BF16),
            pltpu.VMEM((640, 1280), BF16),
            pltpu.VMEM((levels * 16, 1280), BF16),
            pltpu.VMEM((640, levels * 16), F32),
            pltpu.SemaphoreType.DMA,
        ],
        compiler_params=pltpu.CompilerParams(vmem_limit_bytes=20 * 2**20),
        cost_estimate=pl.CostEstimate(flops=6 * 10**9, bytes_accessed=2 * 10**6, transcendentals=0),
        name="pack",
    )(state, owner)


def radiate_kernel(came_ref, depth_ref, out_ref, temp, lost, down, heat):
    blocks, levels, cap = came_ref.shape
    bands = depth_ref.shape[1]
    for j in range(blocks):
        temp[:, j * cap : (j + 1) * cap] = came_ref[j].astype(F32)
    temp[...] = jnp.exp(0.5 * temp[...])
    weight = (iota((bands, 1), 0).astype(F32) + 1.0) * (2.0 / (bands * (bands + 1)))
    flux = jnp.zeros((bands, blocks * cap), F32)
    for level in range(levels):
        share = 1.0 - jnp.exp(-depth_ref[level].astype(F32))
        lost[level] = share
        step = share * (flux - temp[level : level + 1, :])
        down[level] = step
        flux = flux - step
    flux = jnp.broadcast_to(temp[levels - 1 : levels, :], flux.shape)
    for level in reversed(range(levels)):
        step = lost[level] * (flux - temp[level : level + 1, :])
        flux = flux - step
        heat[level : level + 1, :] = jnp.sum(
            (step + down[level]) * weight, axis=0, keepdims=True
        )
    group = out_ref.shape[1]
    for b in range(levels // group):
        out_ref[b] = heat[b * group : (b + 1) * group, :].astype(BF16)


def radiate(came, depth, lat_size, lon_size):
    devices, levels, cap = came.shape
    bands = depth.shape[1]
    width = lon_size * cap
    group = levels // lon_size
    return pl.pallas_call(
        radiate_kernel,
        grid=(lat_size,),
        out_shape=jax.ShapeDtypeStruct((devices, group, width), BF16),
        in_specs=[
            pl.BlockSpec((lon_size, levels, cap), lambda a: (a, 0, 0)),
            pl.BlockSpec((levels, bands, width), lambda a: (0, 0, a)),
        ],
        out_specs=pl.BlockSpec((lon_size, group, width), lambda a: (a, 0, 0)),
        scratch_shapes=[
            pltpu.VMEM((levels, width), F32),
            pltpu.VMEM((levels, bands, width), F32),
            pltpu.VMEM((levels, bands, width), F32),
            pltpu.VMEM((levels, width), F32),
        ],
        compiler_params=pltpu.CompilerParams(vmem_limit_bytes=16 * 2**20),
        name="radiate",
    )(came, depth)


def turns(count, whole):
    quarter = jnp.floor(count * (4.0 / whole) + 0.5)
    angle = (count - quarter * (whole / 4.0)) * (2.0 * math.pi / whole)
    sq = angle * angle
    sin = angle * (1.0 + sq * (-1.0 / 6.0 + sq * (1.0 / 120.0 + sq * (-1.0 / 5040.0))))
    cos = 1.0 + sq * (-0.5 + sq * (1.0 / 24.0 + sq * (-1.0 / 720.0 + sq * (1.0 / 40320.0))))
    side = quarter.astype(I32) & 3
    odd = (side & 1) == 1
    real = jnp.where(odd, sin, cos)
    imag = jnp.where(odd, cos, sin)
    real = jnp.where((side == 1) | (side == 2), -real, real)
    imag = jnp.where(side >= 2, -imag, imag)
    return real, imag


def turned(c, s, rc, rs):
    return c * rc - s * rs, s * rc + c * rs


def fine_kernel(nwave, pair_ref, fine_ref):
    devices = pair_ref.shape[1]
    nlon = fine_ref.shape[3] * 2
    scale = 1.0 / math.sqrt(nlon)
    step_rows = 32
    lane = iota((step_rows, 128), 1)

    def block(i, carry):
        rows = pl.ds(pl.multiple_of(i * step_rows, step_rows), step_rows)
        for h in range(2):
            pair = pair_ref[0, rows, :]
            wave = jnp.where(pair % 2 == h, pair, nwave - 1 - pair).astype(F32)
            wave = jnp.broadcast_to(wave, (step_rows, 128))

            def put(t, c, s):
                fine_ref[0, 2 * h, rows, t * 128 : (t + 1) * 128] = c.astype(BF16)
                fine_ref[0, 2 * h + 1, rows, t * 128 : (t + 1) * 128] = s.astype(BF16)

            c, s = turns(wave * lane.astype(F32), float(nlon))
            c, s = c * scale, s * scale
            r64 = turns(wave * 64.0, float(nlon))
            r128 = turned(*r64, *r64)
            r256 = turned(*r128, *r128)
            r320 = turned(*r256, *r64)
            r512 = turned(*r256, *r256)
            r640 = turned(*r320, *r320)
            low = lane < 64
            last = turned(
                c, s, jnp.where(low, r256[0], r512[0]), jnp.where(low, r256[1], r512[1])
            )
            for t in range(8, 10):
                put(t, *last)
                last = turned(*last, *r640)
            for j in range(4):
                put(2 * j, c, s)
                put(2 * j + 1, *turned(c, s, *r128))
                c, s = turned(c, s, *r320)
        return carry

    lax.fori_loop(0, devices // step_rows, block, 0)


def table(kernel, pairs, nwave, width):
    group, devices, _ = pairs.shape
    size = group * 4 * devices * width
    return pl.pallas_call(
        functools.partial(kernel, nwave),
        grid=(group,),
        out_shape=pltpu.HBM((group, 4, devices, width), BF16),
        in_specs=[pl.BlockSpec((1, devices, 1), lambda s: (s, 0, 0))],
        out_specs=pl.BlockSpec((1, 4, devices, width), lambda s: (s, 0, 0, 0)),
        compiler_params=pltpu.CompilerParams(vmem_limit_bytes=8 * 2**20),
        cost_estimate=pl.CostEstimate(flops=10 * size, bytes_accessed=2 * size, transcendentals=0),
    )(pairs)


def lay_kernel(state_ref, code_ref, out_ref, codes):
    blocks = out_ref.shape[0]
    groups = code_ref.shape[0]
    lines = state_ref.shape[1]
    codes[...] = jnp.zeros_like(codes)
    for g in range(groups):
        code = code_ref[g, :5, :]
        codes[5 * g : 5 * g + 5, :] = (code // 128).astype(F32)
        codes[5 * (groups + g) : 5 * (groups + g) + 5, :] = (code % 128).astype(F32)
    packed = codes[...].astype(BF16)
    for b in range(blocks):
        for level in range(2):
            here = state_ref[2 * b + level].astype(BF16)
            for t in range(2):
                first = (2 * t + level) * lines
                out_ref[b, first : first + lines, :] = here[:, t * 128 : (t + 1) * 128]
            out_ref[b, 4 * lines : 5 * lines, level * 64 : (level + 1) * 64] = here[:, 256:320]
        out_ref[b, 5 * lines :, :] = packed


def lay(state, code, blocks):
    lines = state.shape[1]
    return pl.pallas_call(
        lay_kernel,
        out_shape=jax.ShapeDtypeStruct((blocks, 5 * lines + 104, 128), BF16),
        scratch_shapes=[pltpu.VMEM((104, 128), F32)],
        compiler_params=pltpu.CompilerParams(vmem_limit_bytes=12 * 2**20),
        cost_estimate=pl.CostEstimate(flops=10**6, bytes_accessed=4 * 10**6, transcendentals=0),
        name="lay",
    )(state, code)


def unpack_kernel(came_ref, moved_ref, out_ref, heat):
    blocks, both, devices = came_ref.shape
    levels = 2
    groups = 10
    cap = both // levels
    lines = heat.shape[1] // levels
    first = 400
    own = iota((devices, 128), 0).astype(F32)
    place = iota((cap, 128), 0).astype(F32)

    def block(j, carry):
        table = came_ref[j]
        for g in range(groups):
            marks, ranks = [], []
            for q in range(5):
                row = first + 5 * g + q
                owner = moved_ref[j, row : row + 1, :].astype(F32)
                row += 5 * groups
                ranks.append(moved_ref[j, row : row + 1, :].astype(F32))
                marks.append((own == owner).astype(F32).astype(BF16))
            found = mm(table, jnp.concatenate(marks, axis=1))
            for q in range(5):
                here = place == ranks[q]
                for level in range(levels):
                    part = found[level * cap : (level + 1) * cap, q * 128 : (q + 1) * 128]
                    value = jnp.sum(jnp.where(here, part, 0.0), axis=0, keepdims=True)
                    line = level * lines + 4 * g
                    if q < 4:
                        heat[j, line + q : line + q + 1, :] = value
                    else:
                        tile = blocks + j // 4
                        mine = iota((1, 128), 1) // 32 == j % 4
                        for i in range(4):
                            moved = pltpu.roll(value, (32 * (j % 4 - i) + 128) % 128, 1)
                            old = heat[tile, line + i : line + i + 1, :]
                            heat[tile, line + i : line + i + 1, :] = jnp.where(mine, moved, old)
        return carry

    lax.fori_loop(0, blocks, block, 0)
    for t in range(heat.shape[0]):
        out_ref[:, t * 128 : (t + 1) * 128] = heat[t].astype(BF16)


def unpack(came, moved):
    blocks = came.shape[0]
    shape = (80, blocks * 160)
    return pl.pallas_call(
        unpack_kernel,
        out_shape=jax.ShapeDtypeStruct(shape, BF16),
        scratch_shapes=[pltpu.VMEM((shape[1] // 128, shape[0], 128), F32)],
        compiler_params=pltpu.CompilerParams(vmem_limit_bytes=12 * 2**20),
        name="unpack",
    )(came, moved)


def forward_kernel(nwave, heat_ref, moved_ref, fine_ref, pair_ref, sites_ref, out_ref, rows, mixed):
    step = pl.program_id(0)
    devices = pair_ref.shape[1]
    lines = heat_ref.shape[0]
    cap = lines

    @pl.when(step == 0)
    def _():
        rows[...] = jnp.zeros_like(rows)
        place = iota((256, lines), 0)
        source = (place // 128) * (lines // 2) + (place % 128) // 2
        twice = (source == iota((256, lines), 1)) & (place % 128 < lines)
        double = mm(twice.astype(F32).astype(BF16), heat_ref[...]).astype(BF16)
        wide = (iota((128, 256), 1) // 2 == iota((128, 256), 0)).astype(F32).astype(BF16)
        for t in range(5):
            near, far = (t, t + 4) if t < 4 else (8, 9)
            warm = [mm(double[:, m * 128 : (m + 1) * 128], wide) for m in (near, far)]
            for level in range(2):
                at = slice(level * 128, level * 128 + lines)
                hot = []
                for m, up in zip((near, far), warm):
                    if m < 8:
                        first = [(2 * h + level) * lines for h in range(2)]
                        cold = [moved_ref[m, f : f + lines, :] for f in first]
                    else:
                        side = slice(level * 64, (level + 1) * 64)
                        cold = [
                            moved_ref[4 * (m - 8) + q, 4 * lines : 5 * lines, side]
                            for q in range(4)
                        ]
                    cold = jnp.concatenate([c.astype(F32) for c in cold], axis=1)
                    hot.append(cold + up[at, :])
                span = slice(t * 256, (t + 1) * 256)
                rows[0, at, span] = (hot[0] + hot[1]).astype(BF16)
                rows[1, at, span] = (hot[0] - hot[1]).astype(BF16)

    products = [
        lax.dot_general(
            fine_ref[0, 2 * e : 2 * e + 2].reshape(2 * devices, rows.shape[2]),
            rows[e],
            NT,
            preferred_element_type=F32,
        )
        for e in range(2)
    ]
    pair = pair_ref[0]
    for k in range(4):
        wave = jnp.where(pair % 2 == k // 2, pair, nwave - 1 - pair)
        product = products[k // 2][(k % 2) * devices : (k % 2 + 1) * devices, :]
        part = jnp.where(2 * wave < sites_ref[...], product, 0.0)
        for level in range(2):
            mixed[pl.ds(level * 4 + k, devices, stride=8), :] = part[
                :, level * 128 : (level + 1) * 128
            ]
    for k in range(5):

        @pl.when(step == k)
        def _(k=k):
            out_ref[:, :, k * cap : (k + 1) * cap] = (
                mixed[...].reshape(devices, 8, 128)[:, :, :cap].astype(BF16)
            )


def forward(heat, moved, fine, pairs, sites, nwave):
    group, four, devices, nlon = fine.shape
    return pl.pallas_call(
        functools.partial(forward_kernel, nwave),
        grid=(group,),
        out_shape=jax.ShapeDtypeStruct((devices, 8, group * 80), BF16),
        in_specs=[
            pl.BlockSpec(heat.shape, lambda s: (0, 0)),
            pl.BlockSpec(moved.shape, lambda s: (0, 0, 0)),
            pl.BlockSpec((1, four, devices, nlon), lambda s: (s, 0, 0, 0)),
            pl.BlockSpec((1, devices, 1), lambda s: (s, 0, 0)),
            pl.BlockSpec(sites.shape, lambda s: (0, 0)),
        ],
        out_specs=pl.BlockSpec((devices, 8, group * 80), lambda s: (0, 0, 0)),
        scratch_shapes=[
            pltpu.VMEM((2, 256, nlon), BF16),
            pltpu.VMEM((devices * 8, 128), F32),
        ],
        compiler_params=pltpu.CompilerParams(vmem_limit_bytes=20 * 2**20),
        name="forward",
    )(heat, moved, fine, pairs, sites)


def legendre_kernel(nwave, pair_ref, came_ref, basis_ref, out_ref, held, right, damped, sems):
    group, ndeg, nlat = held.shape
    bands = nlat // 80
    cuts = (0, 512, 1024, ndeg)
    spans = [pl.ds(cuts[q], cuts[q + 1] - cuts[q]) for q in range(3)]

    def copy(s, q):
        return pltpu.make_async_copy(
            basis_ref.at[s, spans[q]], held.at[s, spans[q]], sems.at[s, q]
        )

    for s in range(group):
        for q in range(3):
            copy(s, q).start()

    for s in range(group):
        lanes = slice(s * 80, (s + 1) * 80)
        for a in range(bands):
            block = came_ref[a * 8 : (a + 1) * 8, :, lanes].astype(F32)
            right[s, :, a * 80 : (a + 1) * 80] = block.reshape(64, 80).astype(BF16)
    for s in range(group):
        lanes = slice(s * 80, (s + 1) * 80)
        pair = pair_ref[s]
        for q in range(3):
            copy(s, q).wait()
            size = cuts[q + 1] - cuts[q]
            full = lax.dot_general(
                right[s], held[s, spans[q], :], NT, preferred_element_type=F32
            )
            coeff = iota((64, size), 1) + cuts[q]
            head = (iota((64, size), 0) % 4) // 2 == pair % 2
            first = coeff < nwave - pair
            degree = jnp.where(first, pair + coeff, coeff - 1).astype(F32)
            factor = 1.0 / (1.0 + DIFFUSION * degree * (degree + 1.0) / (nwave * nwave))
            keep = (first & head) | (
                jnp.logical_not(first) & jnp.logical_not(head) & (coeff <= nwave)
            )
            damped[s, :, cuts[q] : cuts[q + 1]] = jnp.where(keep, full * factor, 0.0).astype(
                BF16
            )
        synth = mm(damped[s], held[s])
        for a in range(bands):
            block = synth[:, a * 80 : (a + 1) * 80].reshape(8, 8, 80)
            out_ref[a * 8 : (a + 1) * 8, :, lanes] = block.astype(BF16)


def legendre(pairs, came, basis, nwave):
    group, ndeg, nlat = basis.shape
    return pl.pallas_call(
        functools.partial(legendre_kernel, nwave),
        in_specs=[
            pl.BlockSpec(memory_space=pltpu.SMEM),
            pl.BlockSpec(memory_space=pltpu.VMEM),
            pl.BlockSpec(memory_space=pltpu.HBM),
        ],
        out_specs=pl.BlockSpec(memory_space=pltpu.VMEM),
        scratch_shapes=[
            pltpu.VMEM((group, ndeg, nlat), BF16),
            pltpu.VMEM((group, 64, nlat), BF16),
            pltpu.VMEM((group, 64, ndeg), BF16),
            pltpu.SemaphoreType.DMA((group, 3)),
        ],
        out_shape=jax.ShapeDtypeStruct(came.shape, BF16),
        compiler_params=pltpu.CompilerParams(vmem_limit_bytes=32 * 2**20),
        name="legendre",
    )(pairs, came, basis)


def inverse_kernel(came_ref, fine_ref, out_ref, mixed, left, total):
    step = pl.program_id(0)
    devices = came_ref.shape[0]
    blocks = out_ref.shape[0]
    for k in range(5):

        @pl.when(step == k)
        def _(k=k):
            mixed[:, :80] = (
                came_ref[:, :, k * 80 : (k + 1) * 80].astype(F32).reshape(devices * 8, 80)
            )

    for k in range(4):
        for level in range(2):
            part = mixed[pl.ds(level * 4 + k, devices, stride=8), :]
            left[level * 80 : (level + 1) * 80, k * devices : (k + 1) * devices] = part.T[
                :80, :
            ].astype(BF16)
    half = fine_ref.shape[3]
    for e in range(2):
        product = mm(
            left[:, 2 * e * devices : 2 * (e + 1) * devices],
            fine_ref[0, 2 * e : 2 * e + 2].reshape(2 * devices, half),
        )

        @pl.when(step == 0)
        def _():
            total[e] = product

        @pl.when(step > 0)
        def _():
            total[e] += product

    @pl.when(step == pl.num_programs(0) - 1)
    def _():
        for j in range(blocks):
            k = j % 4
            for t in range(3):
                first = k * 256 + t * 128 if t < 2 else 1024 + k * 64
                span = slice(first, first + (128 if t < 2 else 64))
                even, odd = total[0, :, span], total[1, :, span]
                value = (even + odd if j < 4 else even - odd).astype(BF16)
                if t < 2:
                    out_ref[j, t * 160 : (t + 1) * 160, :] = value
                else:
                    out_ref[j, 320:, :64] = value[:80]
                    out_ref[j, 320:, 64:] = value[80:]


def inverse(came, fine, blocks):
    group, four, devices, half = fine.shape
    return pl.pallas_call(
        inverse_kernel,
        grid=(group,),
        out_shape=jax.ShapeDtypeStruct((blocks, 400, 128), BF16),
        in_specs=[
            pl.BlockSpec(came.shape, lambda s: (0, 0, 0)),
            pl.BlockSpec((1, four, devices, half), lambda s: (s, 0, 0, 0)),
        ],
        out_specs=pl.BlockSpec((blocks, 400, 128), lambda s: (0, 0, 0)),
        scratch_shapes=[
            pltpu.VMEM((devices * 8, 128), F32),
            pltpu.VMEM((160, four * devices), BF16),
            pltpu.VMEM((2, 160, half), F32),
        ],
        compiler_params=pltpu.CompilerParams(vmem_limit_bytes=24 * 2**20),
        name="inverse",
    )(came, fine)


def finish_kernel(came_ref, out_ref):
    lines = out_ref.shape[1]
    for b in range(came_ref.shape[0]):
        for level in range(2):
            for t in range(2):
                first = (2 * t + level) * lines
                out_ref[2 * b + level, :, t * 128 : (t + 1) * 128] = came_ref[
                    b, first : first + lines, :
                ].astype(F32)
            out_ref[2 * b + level, :, 256:] = came_ref[
                b, 4 * lines :, level * 64 : (level + 1) * 64
            ].astype(F32)


def finish(came, levels, lines, width):
    blocks, rows, _ = came.shape
    steps = 2
    return pl.pallas_call(
        finish_kernel,
        grid=(steps,),
        out_shape=jax.ShapeDtypeStruct((levels, lines, width), F32),
        in_specs=[pl.BlockSpec((blocks // steps, rows, 128), lambda s: (s, 0, 0))],
        out_specs=pl.BlockSpec((levels // steps, lines, width), lambda s: (s, 0, 0)),
        compiler_params=pltpu.CompilerParams(vmem_limit_bytes=12 * 2**20),
        name="finish",
    )(came)


def in_hbm(x):
    return pltpu.with_memory_space_constraint(x, pltpu.HBM)


def swap(x, axes):
    return lax.all_to_all(x, axes, split_axis=0, concat_axis=0, tiled=True)


def per_device(state, holder, depths, pairs, sites, basis):
    levels, lines, width = state.shape
    group, _, _ = basis.shape
    nwave = pairs.shape[0] * 2
    nlon = nwave * 2
    lat_size = lax.axis_size("lat")
    lon_size = lax.axis_size("lon")
    devices = lat_size * lon_size
    level_group = levels // lon_size
    rows, cols = lines // 2, width // 2
    me = lax.axis_index("lat") * lon_size + lax.axis_index("lon")
    slots = pairs.reshape(devices, group).T[:, :, None]
    limits = jnp.pad(sites, (0, 128 - lines))
    limits = jnp.concatenate([limits, limits])[None, :]
    owner = jnp.pad(holder.reshape(rows, cols), ((0, 0), (0, 256 - cols)), constant_values=-1)

    sorted_cols, code = pack(state, owner)
    outgoing = sorted_cols.reshape(5, devices, levels, 16).transpose(1, 2, 0, 3)
    came = swap(outgoing.reshape(devices, levels, 80), ALL)
    fine = table(fine_kernel, slots, nwave, nlon // 2)
    laid = lay(state, code, lon_size)
    moved = swap(laid, "lon")
    heat = radiate(came, in_hbm(depths[0]), lat_size, lon_size)
    returned = swap(heat, ALL)
    returned = returned.reshape(devices, level_group, lon_size, 80).transpose(2, 1, 3, 0)
    warm = unpack(returned.reshape(lon_size, level_group * 80, devices), moved)
    sending = forward(warm, moved, in_hbm(fine), slots, limits, nwave)
    arrived = swap(sending, ALL)
    mine = lax.dynamic_slice_in_dim(pairs, me * group, group)
    spread = legendre(mine, arrived, in_hbm(basis.transpose(0, 2, 1)), nwave)
    back = swap(spread, ALL)
    grid = inverse(back, in_hbm(fine), lon_size)
    return finish(swap(grid, "lon"), levels, lines, width)


def solution(mesh):
    in_specs = (
        P(None, "lat", "lon"),
        P(("lat", "lon"), None, None),
        P(("lat", "lon"), None, None, None),
        P(),
        P("lat"),
        P(("lat", "lon"), None, None),
    )
    out_specs = P(None, "lat", "lon")
    return jax.shard_map(
        per_device, mesh=mesh, in_specs=in_specs, out_specs=out_specs, check_vma=False
    )
```

```python
import functools
import math

import jax
import jax.numpy as jnp
from jax import lax
from jax.experimental import pallas as pl
from jax.experimental.pallas import tpu as pltpu
from jax.sharding import PartitionSpec as P


DIFFUSION = 4.0
BF16 = jnp.bfloat16
F32 = jnp.float32
I32 = jnp.int32
ALL = ("lat", "lon")
NT = (((1,), (1,)), ((), ()))


def iota(shape, dim):
    return lax.broadcasted_iota(I32, shape, dim)


def mm(a, b):
    return jnp.dot(a, b, preferred_element_type=F32)


def split_mm_right(x, b):
    hi = x.astype(BF16)
    lo = (x - hi.astype(F32)).astype(BF16)
    return mm(hi, b) + mm(lo, b)


def pack_kernel(
    state_ref, owner_ref, out_ref, code_ref, state, halves, coarse, marks, owners, values, total, sem
):
    levels, lines, width = state_ref.shape
    rows, lanes = owner_ref.shape
    devices = 128
    low = 16
    high = out_ref.shape[0] // devices
    fetch = pltpu.make_async_copy(state_ref, state, sem)
    fetch.start()
    pool_x = (iota((width, lanes), 0) // 2 == iota((width, lanes), 1)).astype(F32).astype(BF16)
    before = (iota((lanes, lanes), 0) < iota((lanes, lanes), 1)).astype(F32).astype(BF16)
    total[...] = jnp.zeros_like(total)
    short = iota((8, 128), 1) < 32

    def tails(x):
        moved = x
        for i in range(1, 4):
            moved = jnp.where(iota((8, 128), 0) % 4 == i, pltpu.roll(x, 32 * i, 1), moved)
        return [jnp.sum(moved[4 * i : 4 * i + 4, :], axis=0, keepdims=True) for i in range(2)]

    def chunk(c, base):
        start = pl.multiple_of(c * 8, 8)
        owner8 = owner_ref[pl.ds(start, 8), :]
        for u in range(8):
            match = (iota((devices, lanes), 0) == owner8[u : u + 1, :]).astype(F32)
            marks[u * devices : (u + 1) * devices, :] = match.astype(BF16)
        counted = mm(marks[...], before)
        ranks = []
        for u in range(8):
            here = counted[u * devices : (u + 1) * devices, :]
            match = (iota((devices, lanes), 0) == owner8[u : u + 1, :]).astype(F32)
            both = jnp.concatenate([base, base], axis=1)
            ranks.append(jnp.sum(match * (here + both), axis=0, keepdims=True))
            base = base + here[:, lanes - 1 : lanes]
        code = owner8 * 128 + jnp.concatenate(ranks, axis=0).astype(I32)
        ends = tails(jnp.where(short, code[:, 128:], 0))
        for i in range(2):
            code_ref[2 * c + i] = jnp.concatenate(
                [code[4 * i : 4 * i + 4, :128], ends[i], jnp.zeros((3, 128), I32)], axis=0
            )
        return base

    def sort(c, carry):
        start = pl.multiple_of(c * 8, 8)
        codes = [code_ref[2 * c + i] for i in range(2)]
        temps = []
        for level in range(levels):
            block = coarse[level, pl.ds(start, 8), :]
            ends = tails(block[:, 128:])
            temps.append(
                [block[4 * i + u : 4 * i + u + 1, :128] if u < 4 else ends[i] for i in range(2) for u in range(5)]
            )
        for u in range(10):
            span = slice(u * 128, (u + 1) * 128)
            code = codes[u // 5][u % 5 : u % 5 + 1, :]
            owner = code // 128
            rank = code % 128
            match = (iota((devices, 128), 0) == owner).astype(F32)
            for h in range(high):
                part = ((rank // low) == h).astype(F32)
                owners[h * devices : (h + 1) * devices, span] = (match * part).astype(BF16)
            slot = (iota((low, 128), 0) == rank % low).astype(F32)
            for level in range(levels):
                values[level * low : (level + 1) * low, span] = (
                    slot * temps[level][u]
                ).astype(BF16)
        total[...] += lax.dot_general(
            owners[...], values[...], NT, preferred_element_type=F32
        )
        return carry

    lax.fori_loop(0, rows // 8, chunk, jnp.zeros((devices, devices), F32))
    fetch.wait()
    summed = split_mm_right(state[...].reshape(levels * lines, width), pool_x)
    for t in range(2):
        halves[t] = summed[:, t * 128 : (t + 1) * 128]
    for level in range(levels):
        for t in range(2):
            even = halves[t, pl.ds(level * lines, rows, stride=2), :]
            odd = halves[t, pl.ds(level * lines + 1, rows, stride=2), :]
            mean = 0.25 * (even + odd)
            coarse[level, :, t * 128 : (t + 1) * 128] = mean.astype(BF16).astype(F32)
    lax.fori_loop(0, rows // 8, sort, 0)
    out_ref[...] = total[...].astype(BF16)


def pack(state, owner):
    levels, lines, _ = state.shape
    rows, lanes = owner.shape
    return pl.pallas_call(
        pack_kernel,
        out_shape=(
            jax.ShapeDtypeStruct((640, levels * 16), BF16),
            jax.ShapeDtypeStruct((rows // 4, 8, 128), I32),
        ),
        in_specs=[
            pl.BlockSpec(memory_space=pltpu.HBM),
            pl.BlockSpec(memory_space=pltpu.VMEM),
        ],
        scratch_shapes=[
            pltpu.VMEM(state.shape, F32),
            pltpu.VMEM((2, levels * lines, 128), F32),
            pltpu.VMEM((levels, rows, lanes), F32),
            pltpu.VMEM((8 * 128, lanes), BF16),
            pltpu.VMEM((640, 1280), BF16),
            pltpu.VMEM((levels * 16, 1280), BF16),
            pltpu.VMEM((640, levels * 16), F32),
            pltpu.SemaphoreType.DMA,
        ],
        compiler_params=pltpu.CompilerParams(vmem_limit_bytes=20 * 2**20),
        cost_estimate=pl.CostEstimate(flops=6 * 10**9, bytes_accessed=2 * 10**6, transcendentals=0),
        name="pack",
    )(state, owner)


def radiate_kernel(came_ref, depth_ref, out_ref, temp, lost, down, heat):
    blocks, levels, cap = came_ref.shape
    bands = depth_ref.shape[1]
    for j in range(blocks):
        temp[:, j * cap : (j + 1) * cap] = came_ref[j].astype(F32)
    temp[...] = jnp.exp(0.5 * temp[...])
    weight = (iota((bands, 1), 0).astype(F32) + 1.0) * (2.0 / (bands * (bands + 1)))
    flux = jnp.zeros((bands, blocks * cap), F32)
    for level in range(levels):
        share = 1.0 - jnp.exp(-depth_ref[level].astype(F32))
        lost[level] = share
        step = share * (flux - temp[level : level + 1, :])
        down[level] = step
        flux = flux - step
    flux = jnp.broadcast_to(temp[levels - 1 : levels, :], flux.shape)
    for level in reversed(range(levels)):
        step = lost[level] * (flux - temp[level : level + 1, :])
        flux = flux - step
        heat[level : level + 1, :] = jnp.sum(
            (step + down[level]) * weight, axis=0, keepdims=True
        )
    group = out_ref.shape[1]
    for b in range(levels // group):
        out_ref[b] = heat[b * group : (b + 1) * group, :].astype(BF16)


def radiate(came, depth, lat_size, lon_size):
    devices, levels, cap = came.shape
    bands = depth.shape[1]
    width = lon_size * cap
    group = levels // lon_size
    return pl.pallas_call(
        radiate_kernel,
        grid=(lat_size,),
        out_shape=jax.ShapeDtypeStruct((devices, group, width), BF16),
        in_specs=[
            pl.BlockSpec((lon_size, levels, cap), lambda a: (a, 0, 0)),
            pl.BlockSpec((levels, bands, width), lambda a: (0, 0, a)),
        ],
        out_specs=pl.BlockSpec((lon_size, group, width), lambda a: (a, 0, 0)),
        scratch_shapes=[
            pltpu.VMEM((levels, width), F32),
            pltpu.VMEM((levels, bands, width), F32),
            pltpu.VMEM((levels, bands, width), F32),
            pltpu.VMEM((levels, width), F32),
        ],
        compiler_params=pltpu.CompilerParams(vmem_limit_bytes=16 * 2**20),
        name="radiate",
    )(came, depth)


def turns(count, whole):
    quarter = jnp.floor(count * (4.0 / whole) + 0.5)
    angle = (count - quarter * (whole / 4.0)) * (2.0 * math.pi / whole)
    sq = angle * angle
    sin = angle * (1.0 + sq * (-1.0 / 6.0 + sq * (1.0 / 120.0 + sq * (-1.0 / 5040.0))))
    cos = 1.0 + sq * (-0.5 + sq * (1.0 / 24.0 + sq * (-1.0 / 720.0 + sq * (1.0 / 40320.0))))
    side = quarter.astype(I32) & 3
    odd = (side & 1) == 1
    real = jnp.where(odd, sin, cos)
    imag = jnp.where(odd, cos, sin)
    real = jnp.where((side == 1) | (side == 2), -real, real)
    imag = jnp.where(side >= 2, -imag, imag)
    return real, imag


def turned(c, s, rc, rs):
    return c * rc - s * rs, s * rc + c * rs


def fine_kernel(nwave, pair_ref, fine_ref):
    devices = pair_ref.shape[1]
    nlon = fine_ref.shape[3] * 2
    scale = 1.0 / math.sqrt(nlon)
    step_rows = 32
    lane = iota((step_rows, 128), 1)

    def block(i, carry):
        rows = pl.ds(pl.multiple_of(i * step_rows, step_rows), step_rows)
        for h in range(2):
            pair = pair_ref[0, rows, :]
            wave = jnp.where(pair % 2 == h, pair, nwave - 1 - pair).astype(F32)
            wave = jnp.broadcast_to(wave, (step_rows, 128))

            def put(t, c, s):
                fine_ref[0, 2 * h, rows, t * 128 : (t + 1) * 128] = c.astype(BF16)
                fine_ref[0, 2 * h + 1, rows, t * 128 : (t + 1) * 128] = s.astype(BF16)

            c, s = turns(wave * lane.astype(F32), float(nlon))
            c, s = c * scale, s * scale
            r64 = turns(wave * 64.0, float(nlon))
            r128 = turned(*r64, *r64)
            r256 = turned(*r128, *r128)
            r320 = turned(*r256, *r64)
            r512 = turned(*r256, *r256)
            r640 = turned(*r320, *r320)
            low = lane < 64
            last = turned(
                c, s, jnp.where(low, r256[0], r512[0]), jnp.where(low, r256[1], r512[1])
            )
            for t in range(8, 10):
                put(t, *last)
                last = turned(*last, *r640)
            for j in range(4):
                put(2 * j, c, s)
                put(2 * j + 1, *turned(c, s, *r128))
                c, s = turned(c, s, *r320)
        return carry

    lax.fori_loop(0, devices // step_rows, block, 0)


def table(kernel, pairs, nwave, width):
    group, devices, _ = pairs.shape
    size = group * 4 * devices * width
    return pl.pallas_call(
        functools.partial(kernel, nwave),
        grid=(group,),
        out_shape=pltpu.HBM((group, 4, devices, width), BF16),
        in_specs=[pl.BlockSpec((1, devices, 1), lambda s: (s, 0, 0))],
        out_specs=pl.BlockSpec((1, 4, devices, width), lambda s: (s, 0, 0, 0)),
        compiler_params=pltpu.CompilerParams(vmem_limit_bytes=8 * 2**20),
        cost_estimate=pl.CostEstimate(flops=10 * size, bytes_accessed=2 * size, transcendentals=0),
    )(pairs)


def lay_kernel(state_ref, code_ref, out_ref, codes):
    blocks = out_ref.shape[0]
    groups = code_ref.shape[0]
    lines = state_ref.shape[1]
    codes[...] = jnp.zeros_like(codes)
    for g in range(groups):
        code = code_ref[g, :5, :]
        codes[5 * g : 5 * g + 5, :] = (code // 128).astype(F32)
        codes[5 * (groups + g) : 5 * (groups + g) + 5, :] = (code % 128).astype(F32)
    packed = codes[...].astype(BF16)
    for b in range(blocks):
        for level in range(2):
            here = state_ref[2 * b + level].astype(BF16)
            for t in range(2):
                first = (2 * t + level) * lines
                out_ref[b, first : first + lines, :] = here[:, t * 128 : (t + 1) * 128]
            out_ref[b, 4 * lines : 5 * lines, level * 64 : (level + 1) * 64] = here[:, 256:320]
        out_ref[b, 5 * lines :, :] = packed


def lay(state, code, blocks):
    lines = state.shape[1]
    return pl.pallas_call(
        lay_kernel,
        out_shape=jax.ShapeDtypeStruct((blocks, 5 * lines + 104, 128), BF16),
        scratch_shapes=[pltpu.VMEM((104, 128), F32)],
        compiler_params=pltpu.CompilerParams(vmem_limit_bytes=12 * 2**20),
        cost_estimate=pl.CostEstimate(flops=10**6, bytes_accessed=4 * 10**6, transcendentals=0),
        name="lay",
    )(state, code)


def unpack_kernel(came_ref, moved_ref, out_ref, heat):
    blocks, both, devices = came_ref.shape
    levels = 2
    groups = 10
    cap = both // levels
    lines = heat.shape[1] // levels
    first = 400
    own = iota((devices, 128), 0).astype(F32)
    place = iota((cap, 128), 0).astype(F32)

    def block(j, carry):
        table = came_ref[j]
        for g in range(groups):
            marks, ranks = [], []
            for q in range(5):
                row = first + 5 * g + q
                owner = moved_ref[j, row : row + 1, :].astype(F32)
                row += 5 * groups
                ranks.append(moved_ref[j, row : row + 1, :].astype(F32))
                marks.append((own == owner).astype(F32).astype(BF16))
            found = mm(table, jnp.concatenate(marks, axis=1))
            for q in range(5):
                here = place == ranks[q]
                for level in range(levels):
                    part = found[level * cap : (level + 1) * cap, q * 128 : (q + 1) * 128]
                    value = jnp.sum(jnp.where(here, part, 0.0), axis=0, keepdims=True)
                    line = level * lines + 4 * g
                    if q < 4:
                        heat[j, line + q : line + q + 1, :] = value
                    else:
                        tile = blocks + j // 4
                        mine = iota((1, 128), 1) // 32 == j % 4
                        for i in range(4):
                            moved = pltpu.roll(value, (32 * (j % 4 - i) + 128) % 128, 1)
                            old = heat[tile, line + i : line + i + 1, :]
                            heat[tile, line + i : line + i + 1, :] = jnp.where(mine, moved, old)
        return carry

    lax.fori_loop(0, blocks, block, 0)
    for t in range(heat.shape[0]):
        out_ref[:, t * 128 : (t + 1) * 128] = heat[t].astype(BF16)


def unpack(came, moved):
    blocks = came.shape[0]
    shape = (80, blocks * 160)
    return pl.pallas_call(
        unpack_kernel,
        out_shape=jax.ShapeDtypeStruct(shape, BF16),
        scratch_shapes=[pltpu.VMEM((shape[1] // 128, shape[0], 128), F32)],
        compiler_params=pltpu.CompilerParams(vmem_limit_bytes=12 * 2**20),
        name="unpack",
    )(came, moved)


def forward_kernel(
    nwave, heat_ref, moved_ref, fine_ref, pair_ref, sites_ref, out_ref, held, rows, mixed, sems
):
    group, _, devices, half = held.shape
    lines = heat_ref.shape[0]
    cap = lines

    def copy(s):
        return pltpu.make_async_copy(fine_ref.at[s], held.at[s], sems.at[s])

    for s in range(group):
        copy(s).start()
    rows[...] = jnp.zeros_like(rows)
    place = iota((256, lines), 0)
    source = (place // 128) * (lines // 2) + (place % 128) // 2
    twice = (source == iota((256, lines), 1)) & (place % 128 < lines)
    double = mm(twice.astype(F32).astype(BF16), heat_ref[...]).astype(BF16)
    wide = (iota((128, 256), 1) // 2 == iota((128, 256), 0)).astype(F32).astype(BF16)
    for t in range(5):
        near, far = (t, t + 4) if t < 4 else (8, 9)
        warm = [mm(double[:, m * 128 : (m + 1) * 128], wide) for m in (near, far)]
        for level in range(2):
            at = slice(level * 128, level * 128 + lines)
            hot = []
            for m, up in zip((near, far), warm):
                if m < 8:
                    first = [(2 * h + level) * lines for h in range(2)]
                    cold = [moved_ref[m, f : f + lines, :] for f in first]
                else:
                    side = slice(level * 64, (level + 1) * 64)
                    cold = [
                        moved_ref[4 * (m - 8) + q, 4 * lines : 5 * lines, side]
                        for q in range(4)
                    ]
                cold = jnp.concatenate([c.astype(F32) for c in cold], axis=1)
                hot.append(cold + up[at, :])
            span = slice(t * 256, (t + 1) * 256)
            rows[0, at, span] = (hot[0] + hot[1]).astype(BF16)
            rows[1, at, span] = (hot[0] - hot[1]).astype(BF16)

    for s in range(group):
        copy(s).wait()
        products = [
            lax.dot_general(
                held[s, 2 * e : 2 * e + 2].reshape(2 * devices, half),
                rows[e],
                NT,
                preferred_element_type=F32,
            )
            for e in range(2)
        ]
        pair = pair_ref[s]
        for k in range(4):
            wave = jnp.where(pair % 2 == k // 2, pair, nwave - 1 - pair)
            product = products[k // 2][(k % 2) * devices : (k % 2 + 1) * devices, :]
            part = jnp.where(2 * wave < sites_ref[...], product, 0.0)
            for level in range(2):
                mixed[s, pl.ds(level * 4 + k, devices, stride=8), :] = part[
                    :, level * 128 : (level + 1) * 128
                ]
        out_ref[:, :, s * cap : (s + 1) * cap] = (
            mixed[s].reshape(devices, 8, 128)[:, :, :cap].astype(BF16)
        )


def forward(heat, moved, fine, pairs, sites, nwave):
    group, _, devices, half = fine.shape
    vmem = pl.BlockSpec(memory_space=pltpu.VMEM)
    return pl.pallas_call(
        functools.partial(forward_kernel, nwave),
        out_shape=jax.ShapeDtypeStruct((devices, 8, group * 80), BF16),
        in_specs=[vmem, vmem, pl.BlockSpec(memory_space=pltpu.HBM), vmem, vmem],
        out_specs=vmem,
        scratch_shapes=[
            pltpu.VMEM(fine.shape, BF16),
            pltpu.VMEM((2, 256, half), BF16),
            pltpu.VMEM((group, devices * 8, 128), F32),
            pltpu.SemaphoreType.DMA((group,)),
        ],
        compiler_params=pltpu.CompilerParams(vmem_limit_bytes=24 * 2**20),
        name="forward",
    )(heat, moved, fine, pairs, sites)


def legendre_kernel(nwave, pair_ref, came_ref, basis_ref, out_ref, held, right, damped, sems):
    group, ndeg, nlat = held.shape
    bands = nlat // 80
    cuts = (0, 512, 1024, ndeg)
    spans = [pl.ds(cuts[q], cuts[q + 1] - cuts[q]) for q in range(3)]

    def copy(s, q):
        return pltpu.make_async_copy(
            basis_ref.at[s, spans[q]], held.at[s, spans[q]], sems.at[s, q]
        )

    for s in range(group):
        for q in range(3):
            copy(s, q).start()

    for s in range(group):
        lanes = slice(s * 80, (s + 1) * 80)
        for a in range(bands):
            block = came_ref[a * 8 : (a + 1) * 8, :, lanes].astype(F32)
            right[s, :, a * 80 : (a + 1) * 80] = block.reshape(64, 80).astype(BF16)
    for s in range(group):
        lanes = slice(s * 80, (s + 1) * 80)
        pair = pair_ref[s]
        for q in range(3):
            copy(s, q).wait()
            size = cuts[q + 1] - cuts[q]
            full = lax.dot_general(
                right[s], held[s, spans[q], :], NT, preferred_element_type=F32
            )
            coeff = iota((64, size), 1) + cuts[q]
            head = (iota((64, size), 0) % 4) // 2 == pair % 2
            first = coeff < nwave - pair
            degree = jnp.where(first, pair + coeff, coeff - 1).astype(F32)
            factor = 1.0 / (1.0 + DIFFUSION * degree * (degree + 1.0) / (nwave * nwave))
            keep = (first & head) | (
                jnp.logical_not(first) & jnp.logical_not(head) & (coeff <= nwave)
            )
            damped[s, :, cuts[q] : cuts[q + 1]] = jnp.where(keep, full * factor, 0.0).astype(
                BF16
            )
        synth = mm(damped[s], held[s])
        for a in range(bands):
            block = synth[:, a * 80 : (a + 1) * 80].reshape(8, 8, 80)
            out_ref[a * 8 : (a + 1) * 8, :, lanes] = block.astype(BF16)


def legendre(pairs, came, basis, nwave):
    group, ndeg, nlat = basis.shape
    return pl.pallas_call(
        functools.partial(legendre_kernel, nwave),
        in_specs=[
            pl.BlockSpec(memory_space=pltpu.SMEM),
            pl.BlockSpec(memory_space=pltpu.VMEM),
            pl.BlockSpec(memory_space=pltpu.HBM),
        ],
        out_specs=pl.BlockSpec(memory_space=pltpu.VMEM),
        scratch_shapes=[
            pltpu.VMEM((group, ndeg, nlat), BF16),
            pltpu.VMEM((group, 64, nlat), BF16),
            pltpu.VMEM((group, 64, ndeg), BF16),
            pltpu.SemaphoreType.DMA((group, 3)),
        ],
        out_shape=jax.ShapeDtypeStruct(came.shape, BF16),
        compiler_params=pltpu.CompilerParams(vmem_limit_bytes=32 * 2**20),
        name="legendre",
    )(pairs, came, basis)


def inverse_kernel(came_ref, fine_ref, out_ref, held, mixed, left, sems):
    _, group, _, devices, half = held.shape
    blocks = out_ref.shape[0]
    wide = 2 * devices

    def copy(e, s):
        return pltpu.make_async_copy(
            fine_ref.at[s, pl.ds(2 * e, 2)], held.at[e, s], sems.at[e, s]
        )

    for e in range(2):
        for s in range(group):
            copy(e, s).start()
    for s in range(group):
        mixed[s, :, :80] = (
            came_ref[:, :, s * 80 : (s + 1) * 80].astype(F32).reshape(devices * 8, 80)
        )
        for k in range(4):
            for level in range(2):
                part = mixed[s, pl.ds(level * 4 + k, devices, stride=8), :]
                first = s * wide + (k % 2) * devices
                left[k // 2, level * 80 : (level + 1) * 80, first : first + devices] = part.T[
                    :80, :
                ].astype(BF16)
    sums = []
    for e in range(2):
        for s in range(group):
            copy(e, s).wait()
        sums.append(mm(left[e], held[e].reshape(group * wide, half)))
    for j in range(blocks):
        k = j % 4
        for t in range(3):
            first = k * 256 + t * 128 if t < 2 else 1024 + k * 64
            span = slice(first, first + (128 if t < 2 else 64))
            even, odd = sums[0][:, span], sums[1][:, span]
            value = (even + odd if j < 4 else even - odd).astype(BF16)
            if t < 2:
                out_ref[j, t * 160 : (t + 1) * 160, :] = value
            else:
                out_ref[j, 320:, :64] = value[:80]
                out_ref[j, 320:, 64:] = value[80:]


def inverse(came, fine, blocks):
    group, _, devices, half = fine.shape
    vmem = pl.BlockSpec(memory_space=pltpu.VMEM)
    return pl.pallas_call(
        inverse_kernel,
        out_shape=jax.ShapeDtypeStruct((blocks, 400, 128), BF16),
        in_specs=[vmem, pl.BlockSpec(memory_space=pltpu.HBM)],
        out_specs=vmem,
        scratch_shapes=[
            pltpu.VMEM((2, group, 2, devices, half), BF16),
            pltpu.VMEM((group, devices * 8, 128), F32),
            pltpu.VMEM((2, 160, group * 2 * devices), BF16),
            pltpu.SemaphoreType.DMA((2, group)),
        ],
        compiler_params=pltpu.CompilerParams(vmem_limit_bytes=24 * 2**20),
        name="inverse",
    )(came, fine)


def finish_kernel(came_ref, out_ref):
    lines = out_ref.shape[1]
    for b in range(came_ref.shape[0]):
        for level in range(2):
            for t in range(2):
                first = (2 * t + level) * lines
                out_ref[2 * b + level, :, t * 128 : (t + 1) * 128] = came_ref[
                    b, first : first + lines, :
                ].astype(F32)
            out_ref[2 * b + level, :, 256:] = came_ref[
                b, 4 * lines :, level * 64 : (level + 1) * 64
            ].astype(F32)


def finish(came, levels, lines, width):
    blocks, rows, _ = came.shape
    steps = 2
    return pl.pallas_call(
        finish_kernel,
        grid=(steps,),
        out_shape=jax.ShapeDtypeStruct((levels, lines, width), F32),
        in_specs=[pl.BlockSpec((blocks // steps, rows, 128), lambda s: (s, 0, 0))],
        out_specs=pl.BlockSpec((levels // steps, lines, width), lambda s: (s, 0, 0)),
        compiler_params=pltpu.CompilerParams(vmem_limit_bytes=12 * 2**20),
        name="finish",
    )(came)


def in_hbm(x):
    return pltpu.with_memory_space_constraint(x, pltpu.HBM)


def swap(x, axes):
    return lax.all_to_all(x, axes, split_axis=0, concat_axis=0, tiled=True)


def per_device(state, holder, depths, pairs, sites, basis):
    levels, lines, width = state.shape
    group, _, _ = basis.shape
    nwave = pairs.shape[0] * 2
    nlon = nwave * 2
    lat_size = lax.axis_size("lat")
    lon_size = lax.axis_size("lon")
    devices = lat_size * lon_size
    level_group = levels // lon_size
    rows, cols = lines // 2, width // 2
    me = lax.axis_index("lat") * lon_size + lax.axis_index("lon")
    slots = pairs.reshape(devices, group).T[:, :, None]
    limits = jnp.pad(sites, (0, 128 - lines))
    limits = jnp.concatenate([limits, limits])[None, :]
    owner = jnp.pad(holder.reshape(rows, cols), ((0, 0), (0, 256 - cols)), constant_values=-1)

    sorted_cols, code = pack(state, owner)
    outgoing = sorted_cols.reshape(5, devices, levels, 16).transpose(1, 2, 0, 3)
    came = swap(outgoing.reshape(devices, levels, 80), ALL)
    fine = table(fine_kernel, slots, nwave, nlon // 2)
    laid = lay(state, code, lon_size)
    moved = swap(laid, "lon")
    heat = radiate(came, in_hbm(depths[0]), lat_size, lon_size)
    returned = swap(heat, ALL)
    returned = returned.reshape(devices, level_group, lon_size, 80).transpose(2, 1, 3, 0)
    warm = unpack(returned.reshape(lon_size, level_group * 80, devices), moved)
    sending = forward(warm, moved, in_hbm(fine), slots, limits, nwave)
    arrived = swap(sending, ALL)
    mine = lax.dynamic_slice_in_dim(pairs, me * group, group)
    spread = legendre(mine, arrived, in_hbm(basis.transpose(0, 2, 1)), nwave)
    back = swap(spread, ALL)
    grid = inverse(back, in_hbm(fine), lon_size)
    return finish(swap(grid, "lon"), levels, lines, width)


def solution(mesh):
    in_specs = (
        P(None, "lat", "lon"),
        P(("lat", "lon"), None, None),
        P(("lat", "lon"), None, None, None),
        P(),
        P("lat"),
        P(("lat", "lon"), None, None),
    )
    out_specs = P(None, "lat", "lon")
    return jax.shard_map(
        per_device, mesh=mesh, in_specs=in_specs, out_specs=out_specs, check_vma=False
    )
```
